256 devices in a mesh: tm: 32 (over z_lo, x, core), cells: 8 (over y, z_hi).
Axes of the slice: x: 4, y: 4, z: 8 (z_hi: 2, z_lo: 4; z = z_hi * 4 + z_lo), core: 2. Of those that a mesh axis runs over, the one named last changes fastest.
Arguments:
- hist_bin: int32 [16384, 8192], P('tm', 'cells'), may hold values from 0 to 255
- obs_bin: int32 [16384, 8192], P('tm', 'cells'), may hold values from 0 to 255
- fut_bin: int32 [16384, 8192], P('tm', 'cells'), may hold values from 0 to 255
- region_id: int32 [8192], P('cells'), may hold values from 0 to 127, as said below
- bin_width: float32 [8192], P('cells'), may hold values from 0.005 to 0.05
- bin_offset: float32 [8192], P('cells'), may hold values from -4 to 4
Outputs:
- adjusted: float32 [16384, 8192], P('tm', 'cells')
The draws below stay inside these ranges and needn't reach their ends.
Inputs may be any that keep to these rules, and one draw needn't show every extreme that they name: `region_id`: every zone of 0 to 127 holds exactly 64 cells.
All inputs are finite; a program needn't handle non-finite values.
Results may differ from the reference program's by a relative error of at most 0.0003.
Values sent between devices are 32-bit elements; how exact they have to be, the bound alone decides.
A program may use at most 64 MiB of HBM per device.

```python
import math
import jax
import jax.numpy as jnp
from jax import lax

BINS = 256
REGIONS = 128
DAYS = 16384
CELLS = 8192


def climate_fields(key):
    zone_key = jax.random.fold_in(key, 11)
    shuffled = jax.random.permutation(zone_key, CELLS).astype(jnp.int32)
    zone_index = (shuffled % REGIONS).astype(jnp.int32)
    regional = jax.random.randint(jax.random.fold_in(key, 12), (REGIONS,), 0, 48)
    jitter = jax.random.randint(jax.random.fold_in(key, 13), (CELLS,), 0, 16)
    model_bias = jax.random.randint(jax.random.fold_in(key, 14), (REGIONS,), -24, 25)
    cell_bias = jax.random.randint(jax.random.fold_in(key, 20), (CELLS,), -40, 41)
    change = jax.random.randint(jax.random.fold_in(key, 15), (REGIONS,), 0, 24)
    season_amp = jax.random.randint(jax.random.fold_in(key, 16), (REGIONS,), 8, 31)
    season_phase = jax.random.randint(jax.random.fold_in(key, 17), (REGIONS,), 0, 365)
    base_slope = jax.random.randint(jax.random.fold_in(key, 18), (REGIONS,), 64, 113)
    future_slope = jax.random.randint(jax.random.fold_in(key, 19), (REGIONS,), 16, 33)
    zone_kind = (jax.random.permutation(jax.random.fold_in(key, 24), REGIONS).astype(jnp.int32) % 4).astype(jnp.int32)
    obs_coarse = (zone_kind == 0)[zone_index]
    hist_coarse = (zone_kind == 1)[zone_index]
    base_shift = regional[zone_index] + jitter
    fields = (season_amp[zone_index], season_phase[zone_index], base_slope[zone_index], future_slope[zone_index])
    return (zone_index, base_shift, model_bias[zone_index] + cell_bias, change[zone_index], fields, obs_coarse, hist_coarse)


def daily_bins(key, salt, shift, fields, extra_slope, coarse):
    season_amp, season_phase, base_slope, future_slope = fields
    days = jnp.arange(DAYS, dtype=jnp.int32)
    phase = (days[:, None] + season_phase[None, :]) % 365
    season = season_amp[None, :] * jnp.abs(2 * phase - 364) // 364
    slope = base_slope + extra_slope * future_slope
    drift = slope[None, :] * days[:, None] // DAYS
    noise_key = jax.random.fold_in(key, salt)
    first_key, second_key, third_key = jax.random.split(noise_key, 3)
    total_noise = jax.random.randint(first_key, (DAYS, CELLS), 0, 33)
    total_noise = total_noise + jax.random.randint(second_key, (DAYS, CELLS), 0, 33)
    total_noise = total_noise + jax.random.randint(third_key, (DAYS, CELLS), 0, 33)
    fine = jnp.clip(shift[None, :] + season + drift + total_noise - 24, 0, BINS - 1).astype(jnp.int32)
    rounded = (2 * (fine // 2)).astype(jnp.int32)
    return jnp.where(coarse[None, :], rounded, fine).astype(jnp.int32)


def draw_hist_bin(key, part):
    zone_index, base_shift, model_bias, change, fields, obs_coarse, hist_coarse = climate_fields(key)
    return daily_bins(key, 21, base_shift + model_bias, fields, 0, hist_coarse)


def draw_obs_bin(key, part):
    zone_index, base_shift, model_bias, change, fields, obs_coarse, hist_coarse = climate_fields(key)
    return daily_bins(key, 22, base_shift, fields, 0, obs_coarse)


def draw_fut_bin(key, part):
    zone_index, base_shift, model_bias, change, fields, obs_coarse, hist_coarse = climate_fields(key)
    never_coarse = jnp.zeros((CELLS,), dtype=bool)
    return daily_bins(key, 23, base_shift + model_bias + change, fields, 1, never_coarse)


def draw_region_id(key, part):
    zone_index, base_shift, model_bias, change, fields, obs_coarse, hist_coarse = climate_fields(key)
    return zone_index.astype(jnp.int32)


def levels(stream_key, dims, shards, least, largest):
    def one(axis_at, parts):
        heights = jax.random.uniform(jax.random.fold_in(jax.random.fold_in(stream_key, 6), axis_at), (parts,), jnp.float32, least / len(shards), largest / len(shards))
        return jnp.repeat(jnp.exp(heights), dims[axis_at] // parts).reshape((-1,) + (1,) * (len(dims) - axis_at - 1))

    level = one(*shards[0])
    for cut in shards[1:]:
        level = level * one(*cut)
    return level


def bell_draw(own_key, shape, spread, bound, shards=(), held_as=jnp.bfloat16):
    values = jax.random.normal(own_key, shape, jnp.float32) * spread
    if len(shards) > 0:
        values = levels(own_key, shape, shards, -0.22, 0.18) * values
    return jnp.clip(values, min=-bound, max=bound).astype(held_as)


def setup_inputs(seed: int = 0) -> dict:
    keys = jax.random.split(jax.random.key(seed), 7)
    hist_bin = draw_hist_bin(jax.random.fold_in(keys[6], 71), 0)
    obs_bin = draw_obs_bin(jax.random.fold_in(keys[6], 71), 0)
    fut_bin = draw_fut_bin(jax.random.fold_in(keys[6], 71), 0)
    region_id = draw_region_id(jax.random.fold_in(keys[6], 71), 0)
    bin_width = jnp.clip(jnp.exp(math.log(0.05) - 2.3025851 * jax.random.uniform(keys[4], (CELLS,), jnp.float32) ** levels(keys[4], (CELLS,), ((0, 8),), -0.2, 0.2)), 0.005, 0.05)
    bin_offset = bell_draw(keys[5], (CELLS,), 1.0, 4.0, ((0, 8),), jnp.float32)
    return {"hist_bin": hist_bin, "obs_bin": obs_bin, "fut_bin": fut_bin, "region_id": region_id, "bin_width": bin_width, "bin_offset": bin_offset}


def count_series(bins_array):
    cell_base = jnp.arange(CELLS, dtype=jnp.int32)[None, :] * BINS
    flat_index = (bins_array + cell_base).reshape(-1)
    tallied = jnp.bincount(flat_index, length=CELLS * BINS)
    return tallied.reshape(CELLS, BINS).astype(jnp.float32)


def quantile_at(rank_rows, before_rows, pooled_rows):
    ramp_terms = jnp.minimum(jnp.maximum(rank_rows[:, :, None] - before_rows[:, None, :], 0.0), pooled_rows[:, None, :])
    return jnp.sum(ramp_terms / jnp.maximum(pooled_rows, 1.0)[:, None, :], axis=2)


def reference(hist_bin, obs_bin, fut_bin, region_id, bin_width, bin_offset):
    counts = jnp.stack([count_series(hist_bin), count_series(obs_bin), count_series(fut_bin)])
    zone_counts = jnp.stack([jax.ops.segment_sum(counts[series_index], region_id, num_segments=REGIONS) for series_index in range(3)])
    zone_share = zone_counts / jnp.sum(zone_counts, axis=2, keepdims=True)
    pooled = counts + (0.5 * DAYS) * zone_share[:, region_id, :]
    running = jnp.cumsum(pooled, axis=2)
    before = running - pooled
    future_rank = before[2] + 0.5 * pooled[2]
    group_size = math.gcd(CELLS, 256)
    group_count = CELLS // group_size

    def per_group(group_rows):
        rank_rows, obs_before, obs_pooled, hist_before, hist_pooled = group_rows
        return quantile_at(rank_rows, obs_before, obs_pooled), quantile_at(rank_rows, hist_before, hist_pooled)

    shaped = (future_rank.reshape(group_count, group_size, BINS), before[1].reshape(group_count, group_size, BINS), pooled[1].reshape(group_count, group_size, BINS), before[0].reshape(group_count, group_size, BINS), pooled[0].reshape(group_count, group_size, BINS))
    quant_obs, quant_hist = lax.map(per_group, shaped)
    quant_obs = quant_obs.reshape(CELLS, BINS)
    quant_hist = quant_hist.reshape(CELLS, BINS)
    centers = (jnp.arange(BINS, dtype=jnp.int32).astype(jnp.float32) + 0.5)[None, :]
    lookup = bin_offset[:, None] + bin_width[:, None] * ((centers + quant_obs) - quant_hist)
    return jnp.take_along_axis(lookup.T, fut_bin, axis=0)
```

```python
import functools

import jax
import jax.numpy as jnp
from jax import lax
from jax.experimental import pallas as pl
from jax.experimental.pallas import tpu as pltpu
from jax.sharding import PartitionSpec as P

BINS = 256
REGIONS = 128
F32 = jnp.float32
BF16 = jnp.bfloat16
POOL_WEIGHT = 0.5

NZ, NX, NK = 4, 4, 2
NC = 8
ROWS = 32


def count_block(xt):
    hi = xt >> 4
    lo = (xt & 15).astype(BF16)
    weight = jnp.where(hi >= 8, 1024.0, 1.0).astype(BF16)
    hi = (hi & 7).astype(BF16)
    zero = jnp.zeros((), BF16)
    one = jnp.ones((), BF16)
    row = lax.broadcasted_iota(jnp.int32, (8, 128), 0)
    lane = lax.broadcasted_iota(jnp.int32, (8, 128), 1)
    slot = lane // 8
    low, high = [], []
    for q in range(8):
        rows = slice(16 * q, 16 * q + 16)
        lo_q, hi_q, w_q = lo[rows], hi[rows], weight[rows]
        lhs = jnp.concatenate([jnp.where(hi_q == float(h), w_q, zero) for h in range(8)], 0)
        rhs = jnp.concatenate([jnp.where(lo_q == float(l), one, zero) for l in range(16)], 0)
        out = lax.dot_general(lhs, rhs, (((1,), (1,)), ((), ())), preferred_element_type=F32)
        for half in range(2):
            idx = (lane % 8) * 16 + half * 8 + row
            packed = jnp.zeros((8, 128), F32)
            for h in range(8):
                for m in range(2):
                    at = 16 * h + 8 * half
                    piece = out[at : at + 8, 128 * m : 128 * m + 128]
                    packed = jnp.where(
                        slot == 2 * h + m, jnp.take_along_axis(piece, idx, axis=1), packed
                    )
            upper = jnp.floor(packed * (1.0 / 1024.0))
            low.append(packed - 1024.0 * upper)
            high.append(upper)
    return jnp.concatenate(low, 0), jnp.concatenate(high, 0)


def hist_kernel(h_ref, o_ref, f_ref, r_ref, c_ref, z_ref):
    @pl.when(pl.program_id(0) == 0)
    def _():
        z_ref[...] = jnp.zeros_like(z_ref)

    zone = lax.broadcasted_iota(jnp.int32, (REGIONS, 128), 0)
    pick = (zone == r_ref[...]).astype(BF16)
    for s, x_ref in enumerate((h_ref, o_ref, f_ref)):
        for half, part in enumerate(count_block(x_ref[...].T)):
            c_ref[s, :, 128 * half : 128 * half + 128] = part
            first = jnp.minimum(part, 256.0)
            rest = part - first
            z_ref[half, s] += jnp.dot(
                pick, first.astype(BF16), preferred_element_type=F32
            ) + jnp.dot(pick, rest.astype(BF16), preferred_element_type=F32)


def histogram(hist_bin, obs_bin, fut_bin, region):
    days, cells = hist_bin.shape
    series = pl.BlockSpec((days, 128), lambda j: (0, j))
    return pl.pallas_call(
        hist_kernel,
        grid=(cells // 128,),
        in_specs=[series, series, series, pl.BlockSpec((1, 128), lambda j: (0, j))],
        out_specs=(
            pl.BlockSpec((3, 128, BINS), lambda j: (0, j, 0)),
            pl.BlockSpec((2, 3, REGIONS, 128), lambda j: (0, 0, 0, 0)),
        ),
        out_shape=(
            jax.ShapeDtypeStruct((3, cells, BINS), F32),
            jax.ShapeDtypeStruct((2, 3, REGIONS, 128), F32),
        ),
        name="hist",
    )(hist_bin, obs_bin, fut_bin, region.reshape(1, cells))


def place():
    me = lax.axis_index("tm")
    k = lax.rem(me, NK)
    x = lax.rem(me // NK, NX)
    z = me // (NK * NX)
    return z, x, k


def tm_of(z, x, k):
    return (z * NX + x) * NK + k


def remote(src, dst, send, recv, tm, cells=None):
    target = {"tm": tm} if cells is None else {"tm": tm, "cells": cells}
    return pltpu.make_async_remote_copy(
        src_ref=src,
        dst_ref=dst,
        send_sem=send,
        recv_sem=recv,
        device_id=target,
        device_id_type=pl.DeviceIdType.MESH,
    )


def greet(partners):
    barrier = pltpu.get_barrier_semaphore()
    for target in partners:
        pl.semaphore_signal(
            barrier, inc=1, device_id=target, device_id_type=pl.DeviceIdType.MESH
        )
    pl.semaphore_wait(barrier, len(partners))


def tm_partners(z, x, k):
    near = [{"tm": tm_of(z, x, 1 - k)}]
    near += [{"tm": tm_of(z, lax.rem(x + j, NX), k)} for j in range(1, NX)]
    near += [{"tm": tm_of(lax.rem(z + j, NZ), x, k)} for j in range(1, NZ)]
    return near


def sum_kernel(
    cnt, zin, tot, zone,
    core_in, acc, far_in, side_in, done, last_in,
    z_core, z_acc, z_x, z_acc2, z_z, z_acc3, z_c,
    s_core, r_core, s_far, r_far, s_side, r_side, s_last, r_last,
    zs_core, zr_core, zs_x, zr_x, zs_z, zr_z, zs_c, zr_c, zs_gz, zr_gz, zs_gx, zr_gx, zs_gk, zr_gk,
):
    z, x, k = place()
    c = lax.axis_index("cells")
    other = tm_of(z, x, 1 - k)
    right = lax.rem(x + 1, NX)
    left = lax.rem(x + NX - 1, NX)
    across = lax.rem(x + 2, NX)
    partners = tm_partners(z, x, k)
    partners += [{"cells": lax.rem(c + j, NC)} for j in range(1, NC)]
    greet(partners)

    def run(copies):
        for copy in copies:
            copy.start()
        return copies

    def drain(copies):
        for copy in copies:
            copy.wait_send()

    zc = run([remote(zin.at[1 - k], z_core, zs_core, zr_core, other)])
    order = (across, right, left, x)
    core = run(
        [
            remote(cnt.at[:, :, at, 1 - k], core_in.at[j], s_core.at[j], r_core.at[j], other)
            for j, at in enumerate(order)
        ]
    )
    zc[0].wait_recv()
    z_acc[...] = zin[k] + z_core[...]
    zx = run(
        [
            remote(z_acc.at[:, :, lax.rem(x + j, NX)], z_x.at[j - 1], zs_x.at[j - 1], zr_x.at[j - 1],
                   tm_of(z, lax.rem(x + j, NX), k))
            for j in range(1, NX)
        ]
    )
    core[0].wait_recv()
    acc[0] = cnt[:, :, across, k] + core_in[0]
    far = run(
        [
            remote(acc.at[0, :, 0:2], far_in.at[0], s_far.at[0], r_far.at[0], tm_of(z, right, k)),
            remote(acc.at[0, :, 2:4], far_in.at[1], s_far.at[1], r_far.at[1], tm_of(z, left, k)),
        ]
    )
    core[1].wait_recv()
    acc[1, :, 2:4] = cnt[:, 2:4, right, k] + core_in[1, :, 2:4]
    side = run([remote(acc.at[1, :, 2:4], side_in.at[0, :, 2:4], s_side.at[0], r_side.at[0], tm_of(z, right, k))])
    core[2].wait_recv()
    acc[2, :, 0:2] = cnt[:, 0:2, left, k] + core_in[2, :, 0:2]
    side += run([remote(acc.at[2, :, 0:2], side_in.at[1, :, 0:2], s_side.at[1], r_side.at[1], tm_of(z, left, k))])

    for copy in zx:
        copy.wait_recv()
    z_acc2[...] = z_acc[:, :, x] + z_x[0] + z_x[1] + z_x[2]
    zz = run(
        [
            remote(z_acc2.at[:, lax.rem(z + j, NZ)], z_z.at[j - 1], zs_z.at[j - 1], zr_z.at[j - 1],
                   tm_of(lax.rem(z + j, NZ), x, k))
            for j in range(1, NZ)
        ]
    )

    far[0].wait_recv()
    acc[1, :, 0:2] = cnt[:, 0:2, right, k] + core_in[1, :, 0:2] + far_in[0]
    side += run([remote(acc.at[1, :, 0:2], side_in.at[0, :, 0:2], s_side.at[2], r_side.at[2], tm_of(z, right, k))])
    far[1].wait_recv()
    acc[2, :, 2:4] = cnt[:, 2:4, left, k] + core_in[2, :, 2:4] + far_in[1]
    side += run([remote(acc.at[2, :, 2:4], side_in.at[1, :, 2:4], s_side.at[3], r_side.at[3], tm_of(z, left, k))])

    for copy in zz:
        copy.wait_recv()
    z_acc3[...] = z_acc2[:, z] + z_z[0] + z_z[1] + z_z[2]
    zg = run(
        [
            remote(z_acc3, z_c.at[j - 1], zs_c.at[j - 1], zr_c.at[j - 1], lax.axis_index("tm"),
                   lax.rem(c + j, NC))
            for j in range(1, NC)
        ]
    )

    core[3].wait_recv()
    acc[3] = cnt[:, :, x, k] + core_in[3]
    side[0].wait_recv()
    side[1].wait_recv()
    side[2].wait_recv()
    side[3].wait_recv()
    done[...] = acc[3] + side_in[0] + side_in[1]
    last = run(
        [
            remote(done.at[:, lax.rem(z + j, NZ)], last_in.at[j - 1], s_last.at[j - 1], r_last.at[j - 1],
                   tm_of(lax.rem(z + j, NZ), x, k))
            for j in range(1, NZ)
        ]
    )

    for copy in zg:
        copy.wait_recv()
    total = z_acc3[...] + z_c[0]
    for j in range(1, NC - 1):
        total = total + z_c[j]
    zone[k, x, z] = total
    gz = run(
        [
            remote(zone.at[k, x, z], zone.at[k, x, z], zs_gz.at[j - 1], zr_gz.at[j - 1],
                   tm_of(lax.rem(z + j, NZ), x, k))
            for j in range(1, NZ)
        ]
    )
    for copy in gz:
        copy.wait_recv()
    gx = run(
        [
            remote(zone.at[k, x], zone.at[k, x], zs_gx.at[j - 1], zr_gx.at[j - 1],
                   tm_of(z, lax.rem(x + j, NX), k))
            for j in range(1, NX)
        ]
    )
    for copy in gx:
        copy.wait_recv()
    gk = run([remote(zone.at[k], zone.at[k], zs_gk, zr_gk, other)])

    for copy in last:
        copy.wait_recv()
    tot[...] = done[:, z] + last_in[0] + last_in[1] + last_in[2]
    gk[0].wait_recv()
    for group in (zc, core, zx, far, side, zz, zg, last, gz, gx, gk):
        drain(group)


def sum_days(counts, zones):
    cnt = counts.reshape(3, NZ, NX, NK, ROWS, BINS)
    zin = zones.reshape(2, 3, NZ, NX, 8, 128)
    vmem = pl.BlockSpec(memory_space=pltpu.VMEM)
    dma = pltpu.SemaphoreType.DMA
    block = (3, NZ, ROWS, BINS)
    return pl.pallas_call(
        sum_kernel,
        out_shape=(
            jax.ShapeDtypeStruct((3, ROWS, BINS), F32),
            jax.ShapeDtypeStruct((NK, NX, NZ, 3, 8, 128), F32),
        ),
        in_specs=[vmem, vmem],
        out_specs=(vmem, vmem),
        scratch_shapes=[
            pltpu.VMEM((4, *block), F32),
            pltpu.VMEM((4, *block), F32),
            pltpu.VMEM((2, 3, 2, ROWS, BINS), F32),
            pltpu.VMEM((2, *block), F32),
            pltpu.VMEM(block, F32),
            pltpu.VMEM((3, 3, ROWS, BINS), F32),
            pltpu.VMEM((3, NZ, NX, 8, 128), F32),
            pltpu.VMEM((3, NZ, NX, 8, 128), F32),
            pltpu.VMEM((3, 3, NZ, 8, 128), F32),
            pltpu.VMEM((3, NZ, 8, 128), F32),
            pltpu.VMEM((3, 3, 8, 128), F32),
            pltpu.VMEM((3, 8, 128), F32),
            pltpu.VMEM((7, 3, 8, 128), F32),
            dma((4,)), dma((4,)), dma((2,)), dma((2,)), dma((4,)), dma((4,)), dma((3,)), dma((3,)),
            dma, dma, dma((3,)), dma((3,)), dma((3,)), dma((3,)), dma((7,)), dma((7,)),
            dma((3,)), dma((3,)), dma((3,)), dma((3,)), dma, dma,
        ],
        compiler_params=pltpu.CompilerParams(
            collective_id=0, has_side_effects=True, vmem_limit_bytes=48 * 2**20
        ),
        name="sum_days",
    )(cnt, zin)


def exact_dot(a, b):
    return jnp.dot(a, b, precision=lax.Precision.HIGHEST, preferred_element_type=F32)


def table_kernel(day_total, tot, zone, reg, wid, off, out, bef, poo, rnk, qnt):
    me = lax.axis_index("tm")
    eye = lax.broadcasted_iota(jnp.int32, (ROWS, ROWS), 0) == lax.broadcasted_iota(
        jnp.int32, (ROWS, ROWS), 1
    )

    def column(ref, zero):
        line = jnp.broadcast_to(ref[pl.ds(me, 1), :], (ROWS, ROWS))
        return jnp.sum(jnp.where(eye, line, zero), axis=1, keepdims=True)

    region = column(reg, 0)
    width = column(wid, 0.0)
    offset = column(off, 0.0)
    pick = (lax.broadcasted_iota(jnp.int32, (ROWS, REGIONS), 1) == region).astype(F32)
    upper = (
        lax.broadcasted_iota(jnp.int32, (BINS, BINS), 0)
        <= lax.broadcasted_iota(jnp.int32, (BINS, BINS), 1)
    ).astype(F32)
    for s in range(3):
        halves = []
        for k in range(NK):
            rows = [zone[k, x, z, s] for z in range(NZ) for x in range(NX)]
            halves.append(jnp.concatenate(rows, 0))
        mine = exact_dot(pick, jnp.concatenate(halves, 1))
        share = mine / jnp.sum(mine, axis=1, keepdims=True)
        pooled = tot[s] + POOL_WEIGHT * day_total * share
        before = exact_dot(pooled, upper) - pooled
        if s < 2:
            bef[s] = before
            poo[s] = pooled
        else:
            rnk[...] = before + 0.5 * pooled

    @pl.loop(0, ROWS // 8)
    def _(i):
        at = pl.ds(pl.multiple_of(i * 8, 8), 8)
        rank = rnk[at, :]
        for s in range(2):
            pooled = poo[s, at, :]
            start = bef[s, at, :].T
            cap = pooled.T
            scale = (1.0 / jnp.maximum(pooled, 1.0)).T
            lines = []
            for c in range(8):
                line = rank[c : c + 1, :]
                total = jnp.zeros((8, BINS), F32)
                for b in range(0, BINS, 8):
                    term = line - start[b : b + 8, c : c + 1]
                    term = jnp.minimum(jnp.maximum(term, 0.0), cap[b : b + 8, c : c + 1])
                    total = total + term * scale[b : b + 8, c : c + 1]
                lines.append(jnp.sum(total, axis=0, keepdims=True))
            qnt[s, at, :] = jnp.concatenate(lines, 0)

    centers = lax.broadcasted_iota(jnp.int32, (ROWS, BINS), 1).astype(F32) + 0.5
    out[...] = offset + width * ((centers + qnt[1]) - qnt[0])


def make_table(tot, zone, region, width, offset, day_total):
    return pl.pallas_call(
        functools.partial(table_kernel, float(day_total)),
        out_shape=jax.ShapeDtypeStruct((ROWS, BINS), F32),
        scratch_shapes=[
            pltpu.VMEM((2, ROWS, BINS), F32),
            pltpu.VMEM((2, ROWS, BINS), F32),
            pltpu.VMEM((ROWS, BINS), F32),
            pltpu.VMEM((2, ROWS, BINS), F32),
        ],
        name="table",
    )(tot, zone, region.reshape(-1, ROWS), width.reshape(-1, ROWS), offset.reshape(-1, ROWS))


def gather_kernel(part, out, sz, rz, sx, rx, sf, rf, sk, rk, own):
    z, x, k = place()
    right = lax.rem(x + 1, NX)
    left = lax.rem(x + NX - 1, NX)
    across = lax.rem(x + 2, NX)
    other = tm_of(z, x, 1 - k)
    greet(tm_partners(z, x, k))
    copy = pltpu.make_async_copy(part, out.at[z, x, k], own)
    copy.start()
    zs = [
        remote(part, out.at[z, x, k], sz.at[j - 1], rz.at[j - 1], tm_of(lax.rem(z + j, NZ), x, k))
        for j in range(1, NZ)
    ]
    for one in zs:
        one.start()
    copy.wait()
    for one in zs:
        one.wait_recv()
    xs = [
        remote(out.at[:, x, k], out.at[:, x, k], sx.at[j], rx.at[j], tm_of(z, at, k))
        for j, at in enumerate((right, left))
    ]
    for one in xs:
        one.start()
    ks = [remote(out.at[:, x, k], out.at[:, x, k], sk.at[0], rk.at[0], other)]
    ks[0].start()
    xs[0].wait_recv()
    xs[1].wait_recv()
    source = lax.rem(x + NX - 1 + 2 * k, NX)
    target = lax.rem(x + 1 + 2 * k, NX)
    forward = remote(out.at[:, source, k], out.at[:, source, k], sf, rf, tm_of(z, target, k))
    forward.start()
    for j, at in enumerate((left, right)):
        one = remote(out.at[:, at, k], out.at[:, at, k], sk.at[1 + j], rk.at[1 + j], other)
        one.start()
        ks.append(one)
    forward.wait_recv()
    one = remote(out.at[:, across, k], out.at[:, across, k], sk.at[3], rk.at[3], other)
    one.start()
    ks.append(one)
    for one in ks:
        one.wait_recv()
    for one in zs + xs + [forward] + ks:
        one.wait_send()


def gather_table(part):
    vmem = pl.BlockSpec(memory_space=pltpu.VMEM)
    dma = pltpu.SemaphoreType.DMA
    return pl.pallas_call(
        gather_kernel,
        out_shape=jax.ShapeDtypeStruct((NZ, NX, NK, ROWS, BINS), F32),
        in_specs=[vmem],
        out_specs=vmem,
        scratch_shapes=[
            dma((3,)), dma((3,)), dma((2,)), dma((2,)), dma, dma, dma((4,)), dma((4,)), dma,
        ],
        compiler_params=pltpu.CompilerParams(collective_id=1, has_side_effects=True),
        name="gather_table",
    )(part)


def apply_kernel(x_ref, t_ref, o_ref):
    xt = x_ref[...].T
    low = t_ref[:, 0:128]
    high = t_ref[:, 128:256]
    for at in range(0, xt.shape[1], 128):
        idx = xt[:, at : at + 128]
        inner = idx & 127
        a = jnp.take_along_axis(low, inner, axis=1)
        b = jnp.take_along_axis(high, inner, axis=1)
        o_ref[at : at + 128, :] = jnp.where(idx >= 128, b, a).T


def apply_table(fut_bin, table):
    days, cells = fut_bin.shape
    return pl.pallas_call(
        apply_kernel,
        grid=(cells // 128,),
        in_specs=[
            pl.BlockSpec((days, 128), lambda j: (0, j)),
            pl.BlockSpec((128, BINS), lambda j: (j, 0)),
        ],
        out_specs=pl.BlockSpec((days, 128), lambda j: (0, j)),
        out_shape=jax.ShapeDtypeStruct((days, cells), F32),
        name="apply",
    )(fut_bin, table)


def body(hist_bin, obs_bin, fut_bin, region_id, bin_width, bin_offset):
    days = hist_bin.shape[0] * lax.axis_size("tm")
    counts, zones = histogram(hist_bin, obs_bin, fut_bin, region_id)
    tot, zone = sum_days(counts, zones)
    part = make_table(tot, zone, region_id, bin_width, bin_offset, days)
    table = gather_table(part)
    return apply_table(fut_bin, table.reshape(-1, BINS))


def solution(mesh):
    placed = (
        P("tm", "cells"),
        P("tm", "cells"),
        P("tm", "cells"),
        P("cells"),
        P("cells"),
        P("cells"),
    )
    return jax.shard_map(
        body, mesh=mesh, in_specs=placed, out_specs=P("tm", "cells"), check_vma=False
    )
```

```python
import functools

import jax
import jax.numpy as jnp
from jax import lax
from jax.experimental import pallas as pl
from jax.experimental.pallas import tpu as pltpu
from jax.sharding import PartitionSpec as P

BINS = 256
REGIONS = 128
F32 = jnp.float32
BF16 = jnp.bfloat16
POOL_WEIGHT = 0.5

NZ, NX, NK = 4, 4, 2
NC = 8
ROWS = 32


def stage_block(bins, planes, slot):
    xt = bins.T
    hi = xt >> 4
    planes[slot, 0] = (xt & 15).astype(BF16)
    planes[slot, 1] = (hi & 7).astype(BF16)
    planes[slot, 2] = jnp.where(hi >= 8, 1024.0, 1.0).astype(BF16)


def count_block(planes, slot):
    zero = jnp.zeros((), BF16)
    one = jnp.ones((), BF16)
    row = lax.broadcasted_iota(jnp.int32, (8, 128), 0)
    lane = lax.broadcasted_iota(jnp.int32, (8, 128), 1)
    column = lane // 8
    low, high = [], []
    for q in range(8):
        rows = slice(16 * q, 16 * q + 16)
        lo, hi, weight = planes[slot, 0, rows], planes[slot, 1, rows], planes[slot, 2, rows]
        lhs = jnp.concatenate([jnp.where(hi == float(h), weight, zero) for h in range(8)], 0)
        rhs = jnp.concatenate([jnp.where(lo == float(l), one, zero) for l in range(16)], 0)
        out = lax.dot_general(lhs, rhs, (((1,), (1,)), ((), ())), preferred_element_type=F32)
        for half in range(2):
            idx = (lane % 8) * 16 + half * 8 + row
            packed = jnp.zeros((8, 128), F32)
            for h in range(8):
                for m in range(2):
                    at = 16 * h + 8 * half
                    piece = out[at : at + 8, 128 * m : 128 * m + 128]
                    packed = jnp.where(
                        column == 2 * h + m, jnp.take_along_axis(piece, idx, axis=1), packed
                    )
            upper = jnp.floor(packed * (1.0 / 1024.0))
            low.append(packed - 1024.0 * upper)
            high.append(upper)
    return jnp.concatenate(low, 0), jnp.concatenate(high, 0)


def exact_dot(a, b):
    return jnp.dot(a, b, precision=lax.Precision.HIGHEST, preferred_element_type=F32)


def pick_lane(table, idx):
    low, high = table[:, 0:128], table[:, 128:256]
    parts = []
    for at in (0, 128):
        want = idx[:, at : at + 128]
        inner = want & 127
        a = jnp.take_along_axis(low, inner, axis=1)
        b = jnp.take_along_axis(high, inner, axis=1)
        parts.append(jnp.where(want >= 128, b, a))
    return jnp.concatenate(parts, 1)


def make_table(day_total, tot, zone, reg, wid, off, out):
    me = lax.axis_index("tm")
    first = lax.rem(me, 128 // ROWS) * ROWS
    eye = lax.broadcasted_iota(jnp.int32, (ROWS, 128), 1) == first + lax.broadcasted_iota(
        jnp.int32, (ROWS, 128), 0
    )

    def column(ref, zero):
        line = jnp.broadcast_to(ref[pl.ds(me // (128 // ROWS), 1), :], (ROWS, 128))
        return jnp.sum(jnp.where(eye, line, zero), axis=1, keepdims=True)

    region = column(reg, 0)
    width = column(wid, 0.0)
    offset = column(off, 0.0)
    pick = (lax.broadcasted_iota(jnp.int32, (ROWS, REGIONS), 1) == region).astype(F32)
    upper = (
        lax.broadcasted_iota(jnp.int32, (BINS, BINS), 0)
        <= lax.broadcasted_iota(jnp.int32, (BINS, BINS), 1)
    ).astype(F32)
    pooled, stacked = [], []
    for s in range(3):
        halves = []
        for k in range(NK):
            rows = [zone[s, k, x, z] for z in range(NZ) for x in range(NX)]
            halves.append(jnp.concatenate(rows, 0))
        mine = exact_dot(pick, jnp.concatenate(halves, 1))
        share = mine / jnp.sum(mine, axis=1, keepdims=True)
        pooled.append(tot[s] + POOL_WEIGHT * day_total * share)
    filled = [pooled[s] / jnp.maximum(pooled[s], 1.0) for s in range(2)]
    sums = exact_dot(jnp.concatenate(pooled + filled, 0), upper)
    ends = [sums[ROWS * s : ROWS * s + ROWS] for s in range(5)]
    rank = ends[2] - pooled[2] + 0.5 * pooled[2]
    quantile = []
    for s in range(2):
        at = jnp.zeros((ROWS, BINS), jnp.int32)
        for bit in (128, 64, 32, 16, 8, 4, 2, 1):
            full = pick_lane(ends[s], at + (bit - 1)) <= rank
            at = jnp.where(full, at + bit, at)
        at = jnp.minimum(at, BINS - 1)
        before = pick_lane(ends[s] - pooled[s], at)
        size = pick_lane(pooled[s], at)
        inside = jnp.minimum(jnp.maximum(rank - before, 0.0), size) / jnp.maximum(size, 1.0)
        quantile.append(pick_lane(ends[3 + s] - filled[s], at) + inside)
    centers = lax.broadcasted_iota(jnp.int32, (ROWS, BINS), 1).astype(F32) + 0.5
    out[...] = offset + width * ((centers + quantile[1]) - quantile[0])


def place():
    me = lax.axis_index("tm")
    k = lax.rem(me, NK)
    x = lax.rem(me // NK, NX)
    z = me // (NK * NX)
    return z, x, k


def tm_of(z, x, k):
    return (z * NX + x) * NK + k


def remote(src, dst, send, recv, tm, cells=None):
    target = {"tm": tm} if cells is None else {"tm": tm, "cells": cells}
    return pltpu.make_async_remote_copy(
        src_ref=src,
        dst_ref=dst,
        send_sem=send,
        recv_sem=recv,
        device_id=target,
        device_id_type=pl.DeviceIdType.MESH,
    )


def greet(partners):
    barrier = pltpu.get_barrier_semaphore()
    for target in partners:
        pl.semaphore_signal(
            barrier, inc=1, device_id=target, device_id_type=pl.DeviceIdType.MESH
        )
    return lambda: pl.semaphore_wait(barrier, len(partners))


def main_kernel(
    day_total, hist, obs, fut, region, width, offset, table, fut_t,
    xbuf, planes, cnt, zin, core_in, acc, far_in, side_in, done, last_in, tot,
    zone, z_core, z_acc, z_x, z_acc2, z_y, z_acc3, z_z,
    s_in, s_core, r_core, s_far, r_far, s_side, r_side, s_last, r_last,
    zs_core, zr_core, zs_x, zr_x, zs_y, zr_y, zs_z, zr_z, zs_gx, zr_gx, zs_gk, zr_gk,
    gs_z, gr_z, gs_r, gr_r, gs_l, gr_l, gs_f, gr_f, gs_k, gr_k,
):
    z, x, k = place()
    c = lax.axis_index("cells")
    tm = lax.axis_index("tm")
    other = tm_of(z, x, 1 - k)
    right = lax.rem(x + 1, NX)
    left = lax.rem(x + NX - 1, NX)
    across = lax.rem(x + 2, NX)
    to_right, to_left = tm_of(z, right, k), tm_of(z, left, k)
    order = (across, right, left, x)

    series = [
        pltpu.make_async_copy(ref, xbuf.at[s], s_in.at[s])
        for s, ref in enumerate((hist, obs, fut))
    ]
    for copy in series:
        copy.start()
    y, z_hi = c // 2, lax.rem(c, 2)
    z_full = z_hi * NZ + z
    along_y = [lax.rem(y + j, 4) * 2 + z_hi for j in range(1, 4)]
    along_z = []
    for j in range(1, 2 * NZ):
        at = lax.rem(z_full + j, 2 * NZ)
        along_z.append((tm_of(lax.rem(at, NZ), x, k), y * 2 + at // NZ))
    partners = [{"tm": other}]
    partners += [{"tm": tm_of(z, lax.rem(x + j, NX), k)} for j in range(1, NX)]
    partners += [{"cells": at} for at in along_y]
    partners += [{"tm": a, "cells": b} for a, b in along_z]
    met = greet(partners)
    zin[...] = jnp.zeros_like(zin)

    blocks = xbuf.shape[2] // 128
    last_block = 3 * blocks - 1

    def stage(n):
        j = lax.rem(n, blocks)
        at = pl.ds(pl.multiple_of(j * 128, 128), 128)
        stage_block(xbuf[n // blocks, :, at], planes, lax.rem(n, 2))

    def count(first, stop):
        def one(n, carry):
            stage(jnp.minimum(n + 1, last_block))
            s = n // blocks
            j = lax.rem(n, blocks)
            zones = lax.broadcasted_iota(jnp.int32, (REGIONS, 128), 0)
            pick = (zones == region[pl.ds(j, 1), :]).astype(BF16)
            for half, part in enumerate(count_block(planes, lax.rem(n, 2))):
                cnt[s, j // 2, pl.ds(lax.rem(j, 2) * 2, 2), :, :, 128 * half : 128 * half + 128] = (
                    part.reshape(2, NK, ROWS, 128)
                )
                head = jnp.minimum(part, 256.0)
                rest = part - head
                zin[s, half] += jnp.dot(
                    pick, head.astype(BF16), preferred_element_type=F32
                ) + jnp.dot(pick, rest.astype(BF16), preferred_element_type=F32)
            return carry

        lax.fori_loop(first, stop, one, 0)

    started = []

    def run(copies):
        for copy in copies:
            copy.start()
        started.extend(copies)
        return copies

    held = {}

    def p0(s):
        held["zc", s] = run([remote(zin.at[s, 1 - k], z_core.at[s], zs_core.at[s], zr_core.at[s], other)])
        held["core", s] = run(
            [
                remote(cnt.at[s, :, at, 1 - k], core_in.at[s, j], s_core.at[s, j], r_core.at[s, j], other)
                for j, at in enumerate(order)
            ]
        )

    def p1(s):
        core = held["core", s]
        core[0].wait_recv()
        acc[s, 0] = cnt[s, :, across, k] + core_in[s, 0]
        held["far", s] = run(
            [
                remote(acc.at[s, 0, 0:2], far_in.at[s, 0], s_far.at[s, 0], r_far.at[s, 0], to_right),
                remote(acc.at[s, 0, 2:4], far_in.at[s, 1], s_far.at[s, 1], r_far.at[s, 1], to_left),
            ]
        )
        core[1].wait_recv()
        acc[s, 1, 2:4] = cnt[s, 2:4, right, k] + core_in[s, 1, 2:4]
        core[2].wait_recv()
        acc[s, 2, 0:2] = cnt[s, 0:2, left, k] + core_in[s, 2, 0:2]
        held["side", s] = run(
            [
                remote(acc.at[s, 1, 2:4], side_in.at[s, 0, 2:4], s_side.at[s, 0], r_side.at[s, 0], to_right),
                remote(acc.at[s, 2, 0:2], side_in.at[s, 1, 0:2], s_side.at[s, 1], r_side.at[s, 1], to_left),
            ]
        )
        core[3].wait_recv()
        acc[s, 3] = cnt[s, :, x, k] + core_in[s, 3]

    def p2(s):
        far = held["far", s]
        far[0].wait_recv()
        acc[s, 1, 0:2] = cnt[s, 0:2, right, k] + core_in[s, 1, 0:2] + far_in[s, 0]
        far[1].wait_recv()
        acc[s, 2, 2:4] = cnt[s, 2:4, left, k] + core_in[s, 2, 2:4] + far_in[s, 1]
        held["side", s] += run(
            [
                remote(acc.at[s, 1, 0:2], side_in.at[s, 0, 0:2], s_side.at[s, 2], r_side.at[s, 2], to_right),
                remote(acc.at[s, 2, 2:4], side_in.at[s, 1, 2:4], s_side.at[s, 3], r_side.at[s, 3], to_left),
            ]
        )

    def p3(s):
        for copy in held["side", s]:
            copy.wait_recv()
        done[s] = acc[s, 3] + side_in[s, 0] + side_in[s, 1]
        held["last", s] = run(
            [
                remote(done.at[s, lax.rem(z + j, NZ)], last_in.at[s, j - 1], s_last.at[s, j - 1],
                       r_last.at[s, j - 1], tm_of(lax.rem(z + j, NZ), x, k))
                for j in range(1, NZ)
            ]
        )

    def p4(s):
        for copy in held["last", s]:
            copy.wait_recv()
        tot[s] = done[s, z] + last_in[s, 0] + last_in[s, 1] + last_in[s, 2]

    def q1(s):
        held["zc", s][0].wait_recv()
        z_acc[s] = zin[s, k].reshape(NZ, NX, 8, 128) + z_core[s].reshape(NZ, NX, 8, 128)
        held["zx", s] = run(
            [
                remote(z_acc.at[s, :, lax.rem(x + j, NX)], z_x.at[s, j - 1], zs_x.at[s, j - 1],
                       zr_x.at[s, j - 1], tm_of(z, lax.rem(x + j, NX), k))
                for j in range(1, NX)
            ]
        )

    def q2(s):
        for copy in held["zx", s]:
            copy.wait_recv()
        z_acc2[s] = z_acc[s, :, x] + z_x[s, 0] + z_x[s, 1] + z_x[s, 2]
        held["zy", s] = run(
            [
                remote(z_acc2.at[s], z_y.at[s, j], zs_y.at[s, j], zr_y.at[s, j], tm, at)
                for j, at in enumerate(along_y)
            ]
        )

    def q3(s):
        for copy in held["zy", s]:
            copy.wait_recv()
        z_acc3[s] = z_acc2[s] + z_y[s, 0] + z_y[s, 1] + z_y[s, 2]
        held["zz", s] = run(
            [
                remote(z_acc3.at[s], z_z.at[s, j], zs_z.at[s, j], zr_z.at[s, j], *at)
                for j, at in enumerate(along_z)
            ]
        )

    def q4(s):
        for copy in held["zz", s]:
            copy.wait_recv()
        total = z_acc3[s]
        for j in range(2 * NZ - 1):
            total = total + z_z[s, j]
        zone[s, k, x] = total
        held["gx", s] = run(
            [
                remote(zone.at[s, k, x], zone.at[s, k, x], zs_gx.at[s, j - 1], zr_gx.at[s, j - 1],
                       tm_of(z, lax.rem(x + j, NX), k))
                for j in range(1, NX)
            ]
        )

    def q5(s):
        for copy in held["gx", s]:
            copy.wait_recv()
        held["gk", s] = run([remote(zone.at[s, k], zone.at[s, k], zs_gk.at[s], zr_gk.at[s], other)])

    def q6(s):
        held["gk", s][0].wait_recv()

    def turn(first, stop):
        for j in range(first, stop):
            fut_t[128 * j : 128 * j + 128, :] = xbuf[2, :, 128 * j : 128 * j + 128].T

    step = blocks // 4
    series[0].wait()
    stage(jnp.int32(0))
    count(0, step)
    series[1].wait()
    count(step, blocks)
    met()
    p0(0)
    for s in (1, 2):
        first = s * blocks
        if s == 1:
            series[2].wait()
        count(first, first + step)
        if s == 2:
            q4(0)
            p4(0)
        q1(s - 1)
        p1(s - 1)
        count(first + step, first + 2 * step)
        if s == 2:
            q5(0)
        q2(s - 1)
        p2(s - 1)
        count(first + 2 * step, first + 3 * step)
        if s == 2:
            q6(0)
        q3(s - 1)
        p3(s - 1)
        count(first + 3 * step, first + blocks)
        p0(s)
    turn(0, 2)
    q1(2)
    p1(2)
    q4(1)
    p4(1)
    turn(2, 4)
    q2(2)
    p2(2)
    q5(1)
    turn(4, 6)
    q3(2)
    p3(2)
    q6(1)
    turn(6, blocks)
    q4(2)
    p4(2)
    q5(2)
    q6(2)

    make_table(day_total, tot, zone, region, width, offset, table.at[z, x, k])

    def piece(z_at, x_at):
        return table.at[z_at, x_at, k]

    def spread(j, z_at):
        held["r", j] = run([remote(piece(z_at, x), piece(z_at, x), gs_r.at[j], gr_r.at[j], to_right)])[0]
        held["l", j] = run([remote(piece(z_at, x), piece(z_at, x), gs_l.at[j], gr_l.at[j], to_left)])[0]
        held["k", j] = run([remote(piece(z_at, x), piece(z_at, x), gs_k.at[j], gr_k.at[j], other)])[0]

    zs = run(
        [
            remote(piece(z, x), piece(z, x), gs_z.at[j - 1], gr_z.at[j - 1],
                   tm_of(lax.rem(z + j, NZ), x, k))
            for j in range(1, NZ)
        ]
    )
    spread(0, z)
    back = [lax.rem(z + NZ - j, NZ) for j in range(NZ)]
    passed = lax.rem(x + NX - 1 + 2 * k, NX)
    onward = tm_of(z, lax.rem(x + 1 + 2 * k, NX), k)

    def relay(j):
        held["r", j].wait_recv()
        held["l", j].wait_recv()
        z_at = back[j]
        held["f", j] = run([remote(piece(z_at, passed), piece(z_at, passed), gs_f.at[j], gr_f.at[j], onward)])[0]
        for i, at in enumerate((left, right)):
            n = 4 + 4 * i + j
            held["k", n] = run([remote(piece(z_at, at), piece(z_at, at), gs_k.at[n], gr_k.at[n], other)])[0]

    def finish(j):
        held["f", j].wait_recv()
        z_at = back[j]
        held["k", 12 + j] = run(
            [remote(piece(z_at, across), piece(z_at, across), gs_k.at[12 + j], gr_k.at[12 + j], other)]
        )[0]

    zs[0].wait_recv()
    spread(1, back[1])
    relay(0)
    zs[1].wait_recv()
    spread(2, back[2])
    zs[2].wait_recv()
    spread(3, back[3])
    relay(1)
    finish(0)
    relay(2)
    finish(1)
    relay(3)
    finish(2)
    finish(3)
    for j in range(4 * NZ):
        held["k", j].wait_recv()
    for copy in started:
        copy.wait_send()


def map_table(hist_bin, obs_bin, fut_bin, region, width, offset, day_total):
    days, cells = hist_bin.shape
    vmem = pl.BlockSpec(memory_space=pltpu.VMEM)
    hbm = pl.BlockSpec(memory_space=pltpu.HBM)
    dma = pltpu.SemaphoreType.DMA
    block = (NZ, ROWS, BINS)
    small = (8, 128)
    return pl.pallas_call(
        functools.partial(main_kernel, float(day_total)),
        out_shape=(
            jax.ShapeDtypeStruct((NZ, NX, NK, ROWS, BINS), F32),
            jax.ShapeDtypeStruct((cells, days), jnp.int32),
        ),
        in_specs=[hbm, hbm, hbm, vmem, vmem, vmem],
        out_specs=(vmem, vmem),
        scratch_shapes=[
            pltpu.VMEM((3, days, cells), jnp.int32),
            pltpu.VMEM((2, 3, 128, days), BF16),
            pltpu.VMEM((3, NZ, NX, NK, ROWS, BINS), F32),
            pltpu.VMEM((3, NK, REGIONS, 128), F32),
            pltpu.VMEM((3, 4, *block), F32),
            pltpu.VMEM((3, 4, *block), F32),
            pltpu.VMEM((3, 2, 2, ROWS, BINS), F32),
            pltpu.VMEM((3, 2, *block), F32),
            pltpu.VMEM((3, *block), F32),
            pltpu.VMEM((3, 3, ROWS, BINS), F32),
            pltpu.VMEM((3, ROWS, BINS), F32),
            pltpu.VMEM((3, NK, NX, NZ, *small), F32),
            pltpu.VMEM((3, REGIONS, 128), F32),
            pltpu.VMEM((3, NZ, NX, *small), F32),
            pltpu.VMEM((3, 3, NZ, *small), F32),
            pltpu.VMEM((3, NZ, *small), F32),
            pltpu.VMEM((3, 3, NZ, *small), F32),
            pltpu.VMEM((3, NZ, *small), F32),
            pltpu.VMEM((3, 7, NZ, *small), F32),
            dma((3,)),
            dma((3, 4)), dma((3, 4)), dma((3, 2)), dma((3, 2)), dma((3, 4)), dma((3, 4)), dma((3, 3)), dma((3, 3)),
            dma((3,)), dma((3,)), dma((3, 3)), dma((3, 3)), dma((3, 3)), dma((3, 3)), dma((3, 7)), dma((3, 7)),
            dma((3, 3)), dma((3, 3)), dma((3,)), dma((3,)),
            dma((3,)), dma((3,)), dma((4,)), dma((4,)), dma((4,)), dma((4,)), dma((4,)), dma((4,)),
            dma((16,)), dma((16,)),
        ],
        compiler_params=pltpu.CompilerParams(
            collective_id=0, has_side_effects=True, vmem_limit_bytes=48 * 2**20
        ),
        name="map_table",
    )(hist_bin, obs_bin, fut_bin, *(a.reshape(-1, 128) for a in (region, width, offset)))


def apply_kernel(x_ref, t_ref, o_ref):
    low = t_ref[:, 0:128]
    high = t_ref[:, 128:256]
    for at in range(0, x_ref.shape[1], 128):
        idx = x_ref[:, at : at + 128]
        inner = idx & 127
        a = jnp.take_along_axis(low, inner, axis=1)
        b = jnp.take_along_axis(high, inner, axis=1)
        o_ref[at : at + 128, :] = jnp.where(idx >= 128, b, a).T


def apply_table(fut_t, table):
    cells, days = fut_t.shape
    return pl.pallas_call(
        apply_kernel,
        grid=(cells // 128,),
        in_specs=[
            pl.BlockSpec((128, days), lambda j: (j, 0)),
            pl.BlockSpec((128, BINS), lambda j: (j, 0)),
        ],
        out_specs=pl.BlockSpec((days, 128), lambda j: (0, j)),
        out_shape=jax.ShapeDtypeStruct((days, cells), F32),
        name="apply",
    )(fut_t, table)


def body(hist_bin, obs_bin, fut_bin, region_id, bin_width, bin_offset):
    days = hist_bin.shape[0] * lax.axis_size("tm")
    table, fut_t = map_table(hist_bin, obs_bin, fut_bin, region_id, bin_width, bin_offset, days)
    return apply_table(fut_t, table.reshape(-1, BINS))


def solution(mesh):
    placed = (
        P("tm", "cells"),
        P("tm", "cells"),
        P("tm", "cells"),
        P("cells"),
        P("cells"),
        P("cells"),
    )
    return jax.shard_map(
        body, mesh=mesh, in_specs=placed, out_specs=P("tm", "cells"), check_vma=False
    )
```

```python
import functools

import jax
import jax.numpy as jnp
from jax import lax
from jax.experimental import pallas as pl
from jax.experimental.pallas import tpu as pltpu
from jax.sharding import PartitionSpec as P

BINS = 256
REGIONS = 128
F32 = jnp.float32
BF16 = jnp.bfloat16
F8 = jnp.float8_e4m3fn
POOL_WEIGHT = 0.5

NZ, NX, NK = 4, 4, 2
NC = 8
ROWS = 32


def stage_block(bins, planes, slot):
    xt = bins.T
    planes[slot, 0] = (xt & 15).astype(BF16)
    planes[slot, 1] = (xt >> 4).astype(BF16)


def count_block(planes, slot):
    zero = jnp.zeros((), BF16)
    one = jnp.ones((), BF16)
    row = lax.broadcasted_iota(jnp.int32, (8, 128), 0)
    lane = lax.broadcasted_iota(jnp.int32, (8, 128), 1)
    second = (lane % 16) >= 8
    slot_of = lane // 16
    idx = (lane % 8) * 16 + ((lane // 8) % 2) * 8 + row
    low, high = [], []
    for q in range(8):
        rows = slice(16 * q, 16 * q + 16)
        lo, hi = planes[slot, 0, rows], planes[slot, 1, rows]
        lhs = jnp.concatenate([jnp.where(hi == float(h), one, zero) for h in range(16)], 0)
        rhs = jnp.concatenate([jnp.where(lo == float(l), one, zero) for l in range(16)], 0)
        out = lax.dot_general(
            lhs.astype(F8), rhs.astype(F8), (((1,), (1,)), ((), ())), preferred_element_type=F32
        )
        out = out[0:128] + 1024.0 * out[128:256]
        parts = []
        for m in range(2):
            part = None
            for h in range(8):
                at = 16 * h
                a = out[at : at + 8, 128 * m : 128 * m + 128]
                b = out[at + 8 : at + 16, 128 * m : 128 * m + 128]
                own = jnp.take_along_axis(jnp.where(second, b, a), idx, axis=1)
                part = own if h == 0 else jnp.where(slot_of == h, own, part)
            parts.append(part)
        for packed in (
            jnp.where(second, pltpu.roll(parts[1], 8, 1), parts[0]),
            jnp.where(second, parts[1], pltpu.roll(parts[0], 120, 1)),
        ):
            upper = jnp.floor(packed * (1.0 / 1024.0))
            low.append(packed - 1024.0 * upper)
            high.append(upper)
    return jnp.concatenate(low, 0), jnp.concatenate(high, 0)


def exact_dot(a, b):
    return jnp.dot(a, b, precision=lax.Precision.HIGHEST, preferred_element_type=F32)


def pick_lane(table, idx):
    low, high = table[:, 0:128], table[:, 128:256]
    parts = []
    for at in (0, 128):
        want = idx[:, at : at + 128]
        inner = want & 127
        a = jnp.take_along_axis(low, inner, axis=1)
        b = jnp.take_along_axis(high, inner, axis=1)
        parts.append(jnp.where(want >= 128, b, a))
    return jnp.concatenate(parts, 1)


def make_table(day_total, tot, zone, reg, wid, off, out):
    me = lax.axis_index("tm")
    first = lax.rem(me, 128 // ROWS) * ROWS
    eye = lax.broadcasted_iota(jnp.int32, (ROWS, 128), 1) == first + lax.broadcasted_iota(
        jnp.int32, (ROWS, 128), 0
    )

    def column(ref, zero):
        line = jnp.broadcast_to(ref[pl.ds(me // (128 // ROWS), 1), :], (ROWS, 128))
        return jnp.sum(jnp.where(eye, line, zero), axis=1, keepdims=True)

    region = column(reg, 0)
    width = column(wid, 0.0)
    offset = column(off, 0.0)
    pick = (lax.broadcasted_iota(jnp.int32, (ROWS, REGIONS), 1) == region).astype(F32)
    upper = (
        lax.broadcasted_iota(jnp.int32, (BINS, BINS), 0)
        <= lax.broadcasted_iota(jnp.int32, (BINS, BINS), 1)
    ).astype(F32)
    pooled, stacked = [], []
    for s in range(3):
        mine = exact_dot(pick, jnp.concatenate([zone[s, k].reshape(REGIONS, 128) for k in range(NK)], 1))
        share = mine / jnp.sum(mine, axis=1, keepdims=True)
        pooled.append(tot[s] + POOL_WEIGHT * day_total * share)
    filled = [pooled[s] / jnp.maximum(pooled[s], 1.0) for s in range(2)]
    sums = exact_dot(jnp.concatenate(pooled + filled, 0), upper)
    ends = [sums[ROWS * s : ROWS * s + ROWS] for s in range(5)]
    rank = ends[2] - pooled[2] + 0.5 * pooled[2]
    quantile = []
    for s in range(2):
        at = jnp.zeros((ROWS, BINS), jnp.int32)
        for bit in (128, 64, 32, 16, 8, 4, 2, 1):
            full = pick_lane(ends[s], at + (bit - 1)) <= rank
            at = jnp.where(full, at + bit, at)
        at = jnp.minimum(at, BINS - 1)
        before = pick_lane(ends[s] - pooled[s], at)
        size = pick_lane(pooled[s], at)
        inside = jnp.minimum(jnp.maximum(rank - before, 0.0), size) / jnp.maximum(size, 1.0)
        quantile.append(pick_lane(ends[3 + s] - filled[s], at) + inside)
    centers = lax.broadcasted_iota(jnp.int32, (ROWS, BINS), 1).astype(F32) + 0.5
    out[...] = offset + width * ((centers + quantile[1]) - quantile[0])


def place():
    me = lax.axis_index("tm")
    k = lax.rem(me, NK)
    x = lax.rem(me // NK, NX)
    z = me // (NK * NX)
    return z, x, k


def tm_of(z, x, k):
    return (z * NX + x) * NK + k


def remote(src, dst, send, recv, tm, cells=None):
    target = {"tm": tm} if cells is None else {"tm": tm, "cells": cells}
    return pltpu.make_async_remote_copy(
        src_ref=src,
        dst_ref=dst,
        send_sem=send,
        recv_sem=recv,
        device_id=target,
        device_id_type=pl.DeviceIdType.MESH,
    )


def greet(partners):
    barrier = pltpu.get_barrier_semaphore()
    for target in partners:
        pl.semaphore_signal(
            barrier, inc=1, device_id=target, device_id_type=pl.DeviceIdType.MESH
        )
    return lambda: pl.semaphore_wait(barrier, len(partners))


def main_kernel(
    day_total, hist, obs, fut, reg_in, wid_in, off_in, table, fut_t, reg, wid, off,
    xbuf, planes, cnt, zin, core_in, acc, far_in, side_in, done, last_in, tot,
    zone, z_core, z_acc, z_x, z_acc2, z_z,
    s_in, s_core, r_core, s_far, r_far, s_side, r_side, s_last, r_last,
    zs_core, zr_core, zs_x, zr_x, zs_z, zr_z, zs_gx, zr_gx, zs_gk, zr_gk,
    gs_z, gr_z, gs_r, gr_r, gs_l, gr_l, gs_f, gr_f, gs_k, gr_k,
):
    z, x, k = place()
    c = lax.axis_index("cells")
    tm = lax.axis_index("tm")
    other = tm_of(z, x, 1 - k)
    right = lax.rem(x + 1, NX)
    left = lax.rem(x + NX - 1, NX)
    across = lax.rem(x + 2, NX)
    to_right, to_left = tm_of(z, right, k), tm_of(z, left, k)
    order = (across, right, left, x)

    lead = pltpu.make_async_copy(hist.at[:, 0:128], xbuf.at[0, :, 0:128], s_in.at[0])
    lead.start()
    small = [
        pltpu.make_async_copy(ref, to, s_in.at[4 + i])
        for i, (ref, to) in enumerate(((reg_in, reg), (wid_in, wid), (off_in, off)))
    ]
    small[0].start()
    series = [pltpu.make_async_copy(hist.at[:, 128:], xbuf.at[0, :, 128:], s_in.at[1])]
    series += [
        pltpu.make_async_copy(ref, xbuf.at[s], s_in.at[1 + s]) for s, ref in ((1, obs), (2, fut))
    ]
    for copy in series + small[1:]:
        copy.start()
    y, z_hi = c // 2, lax.rem(c, 2)
    z_full = z_hi * NZ + z
    plane = x * 4 + y
    across_plane = [lax.rem(plane + j, 16) for j in range(1, 16)]
    in_plane = [(tm_of(z, at // 4, k), lax.rem(at, 4) * 2 + z_hi) for at in across_plane]
    along_z = []
    for j in range(1, 2 * NZ):
        at = lax.rem(z_full + j, 2 * NZ)
        along_z.append((tm_of(lax.rem(at, NZ), x, k), y * 2 + at // NZ))
    partners = [{"tm": other}]
    partners += [{"tm": a, "cells": b} for a, b in in_plane + along_z]
    met = greet(partners)
    zin[...] = jnp.zeros_like(zin)

    blocks = xbuf.shape[2] // 128
    last_block = 3 * blocks - 1

    def stage(n):
        j = lax.rem(n, blocks)
        at = pl.ds(pl.multiple_of(j * 128, 128), 128)
        stage_block(xbuf[n // blocks, :, at], planes, lax.rem(n, 2))

    def count(first, stop):
        def one(n, carry):
            stage(jnp.minimum(n + 1, last_block))
            s = n // blocks
            j = lax.rem(n, blocks)
            zones = lax.broadcasted_iota(jnp.int32, (REGIONS, 128), 0)
            pick = (zones == reg[pl.ds(j, 1), :]).astype(BF16)
            counts = count_block(planes, lax.rem(n, 2))
            heads, rests = [], []
            for half, part in enumerate(counts):
                cnt[s, j // 2, pl.ds(lax.rem(j, 2) * 2, 2), :, :, 128 * half : 128 * half + 128] = (
                    part.reshape(2, NK, ROWS, 128)
                )
                head = jnp.minimum(part, 256.0)
                heads.append(head.astype(BF16))
                rests.append((part - head).astype(BF16))
            both = jnp.concatenate(
                [jnp.concatenate(heads, 1), jnp.concatenate(rests, 1)], 0
            )
            sums = jnp.dot(
                jnp.concatenate([pick, pick], 1), both, preferred_element_type=F32
            )
            zin[s, 0] += sums[:, 0:128]
            zin[s, 1] += sums[:, 128:256]
            return carry

        lax.fori_loop(first, stop, one, 0)

    started = []

    def run(copies):
        for copy in copies:
            copy.start()
        started.extend(copies)
        return copies

    held = {}

    def p0(s):
        held["zc", s] = run([remote(zin.at[s, 1 - k], z_core.at[s], zs_core.at[s], zr_core.at[s], other)])
        held["core", s] = run(
            [
                remote(cnt.at[s, :, at, 1 - k], core_in.at[s, j], s_core.at[s, j], r_core.at[s, j], other)
                for j, at in enumerate(order)
            ]
        )

    def p1(s):
        core = held["core", s]
        core[0].wait_recv()
        acc[s, 0] = cnt[s, :, across, k] + core_in[s, 0]
        held["far", s] = run(
            [
                remote(acc.at[s, 0, 0:2], far_in.at[s, 0], s_far.at[s, 0], r_far.at[s, 0], to_right),
                remote(acc.at[s, 0, 2:4], far_in.at[s, 1], s_far.at[s, 1], r_far.at[s, 1], to_left),
            ]
        )
        core[1].wait_recv()
        acc[s, 1, 2:4] = cnt[s, 2:4, right, k] + core_in[s, 1, 2:4]
        core[2].wait_recv()
        acc[s, 2, 0:2] = cnt[s, 0:2, left, k] + core_in[s, 2, 0:2]
        held["side", s] = run(
            [
                remote(acc.at[s, 1, 2:4], side_in.at[s, 0, 2:4], s_side.at[s, 0], r_side.at[s, 0], to_right),
                remote(acc.at[s, 2, 0:2], side_in.at[s, 1, 0:2], s_side.at[s, 1], r_side.at[s, 1], to_left),
            ]
        )
        core[3].wait_recv()
        acc[s, 3] = cnt[s, :, x, k] + core_in[s, 3]

    def p2(s):
        far = held["far", s]
        far[0].wait_recv()
        acc[s, 1, 0:2] = cnt[s, 0:2, right, k] + core_in[s, 1, 0:2] + far_in[s, 0]
        far[1].wait_recv()
        acc[s, 2, 2:4] = cnt[s, 2:4, left, k] + core_in[s, 2, 2:4] + far_in[s, 1]
        held["side", s] += run(
            [
                remote(acc.at[s, 1, 0:2], side_in.at[s, 0, 0:2], s_side.at[s, 2], r_side.at[s, 2], to_right),
                remote(acc.at[s, 2, 2:4], side_in.at[s, 1, 2:4], s_side.at[s, 3], r_side.at[s, 3], to_left),
            ]
        )

    def p3(s):
        for copy in held["side", s]:
            copy.wait_recv()
        done[s] = acc[s, 3] + side_in[s, 0] + side_in[s, 1]
        held["last", s] = run(
            [
                remote(done.at[s, lax.rem(z + j, NZ)], last_in.at[s, j - 1], s_last.at[s, j - 1],
                       r_last.at[s, j - 1], tm_of(lax.rem(z + j, NZ), x, k))
                for j in range(1, NZ)
            ]
        )

    def p4(s):
        for copy in held["last", s]:
            copy.wait_recv()
        tot[s] = done[s, z] + last_in[s, 0] + last_in[s, 1] + last_in[s, 2]

    def q1(s):
        held["zc", s][0].wait_recv()
        z_acc[s] = (zin[s, k] + z_core[s]).reshape(16, 8, 128)
        held["zx", s] = run(
            [
                remote(z_acc.at[s, at], z_x.at[s, j], zs_x.at[s, j], zr_x.at[s, j], *in_plane[j])
                for j, at in enumerate(across_plane)
            ]
        )

    def q2(s):
        for copy in held["zx", s]:
            copy.wait_recv()
        total = z_acc[s, plane]
        for j in range(15):
            total = total + z_x[s, j]
        z_acc2[s] = total

    def q3(s):
        held["zz", s] = run(
            [
                remote(z_acc2.at[s], z_z.at[s, j], zs_z.at[s, j], zr_z.at[s, j], *at)
                for j, at in enumerate(along_z)
            ]
        )

    def q4(s):
        for copy in held["zz", s]:
            copy.wait_recv()
        total = z_acc2[s]
        for j in range(2 * NZ - 1):
            total = total + z_z[s, j]
        zone[s, k, plane] = total

    def q5(s):
        held["gx", s] = run(
            [
                remote(zone.at[s, k, plane], zone.at[s, k, plane], zs_gx.at[s, j], zr_gx.at[s, j], *at)
                for j, at in enumerate(in_plane)
            ]
        )

    def q55(s):
        for copy in held["gx", s]:
            copy.wait_recv()
        held["gk", s] = run([remote(zone.at[s, k], zone.at[s, k], zs_gk.at[s], zr_gk.at[s], other)])

    def q6(s):
        held["gk", s][0].wait_recv()

    def turn(first, stop):
        for j in range(first, stop):
            fut_t[128 * j : 128 * j + 128, :] = xbuf[2, :, 128 * j : 128 * j + 128].T

    step = blocks // 4
    lead.wait()
    stage(jnp.int32(0))
    small[0].wait()
    series[0].wait()
    count(0, step)
    series[1].wait()
    count(step, blocks)
    met()
    p0(0)
    for s in (1, 2):
        first = s * blocks
        if s == 1:
            series[2].wait()
        count(first, first + step)
        if s == 2:
            p4(0)
        q1(s - 1)
        p1(s - 1)
        count(first + step, first + 2 * step)
        if s == 2:
            q55(0)
        q2(s - 1)
        q3(s - 1)
        p2(s - 1)
        count(first + 2 * step, first + 3 * step)
        if s == 2:
            q6(0)
        p3(s - 1)
        count(first + 3 * step, first + blocks)
        p0(s)
        q4(s - 1)
        q5(s - 1)
    q1(2)
    p1(2)
    p4(1)
    turn(0, 4)
    q2(2)
    q3(2)
    p2(2)
    q55(1)
    turn(4, blocks)
    p3(2)
    q4(2)
    q5(2)
    p4(2)
    q6(1)
    small[1].wait()
    small[2].wait()
    q55(2)
    q6(2)

    make_table(day_total, tot, zone, reg, wid, off, table.at[z, x, k])

    def piece(z_at, x_at):
        return table.at[z_at, x_at, k]

    def spread(j, z_at):
        held["r", j] = run([remote(piece(z_at, x), piece(z_at, x), gs_r.at[j], gr_r.at[j], to_right)])[0]
        held["l", j] = run([remote(piece(z_at, x), piece(z_at, x), gs_l.at[j], gr_l.at[j], to_left)])[0]
        held["k", j] = run([remote(piece(z_at, x), piece(z_at, x), gs_k.at[j], gr_k.at[j], other)])[0]

    zs = run(
        [
            remote(piece(z, x), piece(z, x), gs_z.at[j - 1], gr_z.at[j - 1],
                   tm_of(lax.rem(z + j, NZ), x, k))
            for j in range(1, NZ)
        ]
    )
    spread(0, z)
    back = [lax.rem(z + NZ - j, NZ) for j in range(NZ)]
    passed = lax.rem(x + NX - 1 + 2 * k, NX)
    onward = tm_of(z, lax.rem(x + 1 + 2 * k, NX), k)

    def relay(j):
        held["r", j].wait_recv()
        held["l", j].wait_recv()
        z_at = back[j]
        held["f", j] = run([remote(piece(z_at, passed), piece(z_at, passed), gs_f.at[j], gr_f.at[j], onward)])[0]
        for i, at in enumerate((left, right)):
            n = 4 + 4 * i + j
            held["k", n] = run([remote(piece(z_at, at), piece(z_at, at), gs_k.at[n], gr_k.at[n], other)])[0]

    def finish(j):
        held["f", j].wait_recv()
        z_at = back[j]
        held["k", 12 + j] = run(
            [remote(piece(z_at, across), piece(z_at, across), gs_k.at[12 + j], gr_k.at[12 + j], other)]
        )[0]

    zs[0].wait_recv()
    spread(1, back[1])
    relay(0)
    zs[1].wait_recv()
    spread(2, back[2])
    zs[2].wait_recv()
    spread(3, back[3])
    relay(1)
    finish(0)
    relay(2)
    finish(1)
    relay(3)
    finish(2)
    finish(3)
    for j in range(4 * NZ):
        held["k", j].wait_recv()
    for copy in started:
        copy.wait_send()


def map_table(hist_bin, obs_bin, fut_bin, region, width, offset, day_total):
    days, cells = hist_bin.shape
    vmem = pl.BlockSpec(memory_space=pltpu.VMEM)
    hbm = pl.BlockSpec(memory_space=pltpu.HBM)
    dma = pltpu.SemaphoreType.DMA
    block = (NZ, ROWS, BINS)
    small = (8, 128)
    return pl.pallas_call(
        functools.partial(main_kernel, float(day_total)),
        out_shape=(
            jax.ShapeDtypeStruct((NZ, NX, NK, ROWS, BINS), F32),
            jax.ShapeDtypeStruct((cells, days), jnp.int32),
        ),
        in_specs=[hbm] * 6,
        out_specs=(vmem, vmem),
        scratch_shapes=[
            pltpu.VMEM((8, 128), jnp.int32),
            pltpu.VMEM((8, 128), F32),
            pltpu.VMEM((8, 128), F32),
            pltpu.VMEM((3, days, cells), jnp.int32),
            pltpu.VMEM((2, 2, 128, days), BF16),
            pltpu.VMEM((3, NZ, NX, NK, ROWS, BINS), F32),
            pltpu.VMEM((3, NK, REGIONS, 128), F32),
            pltpu.VMEM((3, 4, *block), F32),
            pltpu.VMEM((3, 4, *block), F32),
            pltpu.VMEM((3, 2, 2, ROWS, BINS), F32),
            pltpu.VMEM((3, 2, *block), F32),
            pltpu.VMEM((3, *block), F32),
            pltpu.VMEM((3, 3, ROWS, BINS), F32),
            pltpu.VMEM((3, ROWS, BINS), F32),
            pltpu.VMEM((3, NK, 16, *small), F32),
            pltpu.VMEM((3, REGIONS, 128), F32),
            pltpu.VMEM((3, 16, *small), F32),
            pltpu.VMEM((3, 15, *small), F32),
            pltpu.VMEM((3, *small), F32),
            pltpu.VMEM((3, 7, *small), F32),
            dma((7,)),
            dma((3, 4)), dma((3, 4)), dma((3, 2)), dma((3, 2)), dma((3, 4)), dma((3, 4)), dma((3, 3)), dma((3, 3)),
            dma((3,)), dma((3,)), dma((3, 15)), dma((3, 15)), dma((3, 7)), dma((3, 7)),
            dma((3, 15)), dma((3, 15)), dma((3,)), dma((3,)),
            dma((3,)), dma((3,)), dma((4,)), dma((4,)), dma((4,)), dma((4,)), dma((4,)), dma((4,)),
            dma((16,)), dma((16,)),
        ],
        compiler_params=pltpu.CompilerParams(
            collective_id=0, has_side_effects=True, vmem_limit_bytes=58 * 2**20
        ),
        name="map_table",
    )(hist_bin, obs_bin, fut_bin, *(a.reshape(-1, 128) for a in (region, width, offset)))


APPLY = 256


def apply_kernel(x_ref, t_ref, o_ref):
    rows = pl.ds(pl.multiple_of(pl.program_id(0) * APPLY, APPLY), APPLY)
    low = t_ref[rows, 0:128]
    high = t_ref[rows, 128:256]
    for at in range(0, x_ref.shape[1], 128):
        idx = x_ref[rows, at : at + 128]
        inner = idx & 127
        a = jnp.take_along_axis(low, inner, axis=1)
        b = jnp.take_along_axis(high, inner, axis=1)
        o_ref[at : at + 128, :] = jnp.where(idx >= 128, b, a).T


def apply_table(fut_t, table):
    cells, days = fut_t.shape
    vmem = pl.BlockSpec(memory_space=pltpu.VMEM)
    return pl.pallas_call(
        apply_kernel,
        grid=(cells // APPLY,),
        in_specs=[vmem, vmem],
        out_specs=pl.BlockSpec((days, APPLY), lambda j: (0, j)),
        out_shape=jax.ShapeDtypeStruct((days, cells), F32),
        name="apply",
    )(fut_t, table)


def body(hist_bin, obs_bin, fut_bin, region_id, bin_width, bin_offset):
    days = hist_bin.shape[0] * lax.axis_size("tm")
    table, fut_t = map_table(hist_bin, obs_bin, fut_bin, region_id, bin_width, bin_offset, days)
    return apply_table(fut_t, table.reshape(-1, BINS))


def solution(mesh):
    placed = (
        P("tm", "cells"),
        P("tm", "cells"),
        P("tm", "cells"),
        P("cells"),
        P("cells"),
        P("cells"),
    )
    return jax.shard_map(
        body, mesh=mesh, in_specs=placed, out_specs=P("tm", "cells"), check_vma=False
    )
```

```python
import functools

import jax
import jax.numpy as jnp
from jax import lax
from jax.experimental import pallas as pl
from jax.experimental.pallas import tpu as pltpu
from jax.sharding import PartitionSpec as P

BINS = 256
REGIONS = 128
F32 = jnp.float32
BF16 = jnp.bfloat16
F8 = jnp.float8_e4m3fn
POOL_WEIGHT = 0.5

NZ, NX, NK = 4, 4, 2
NC = 8
ROWS = 32


def stage_block(bins, planes, slot):
    xt = bins.T
    less = (lax.broadcasted_iota(jnp.int32, (32, bins.shape[0]), 0) >= 16).astype(jnp.int32)
    for q in range(8):
        rows = xt[16 * q : 16 * q + 16]
        twice = jnp.concatenate([rows, rows], 0)
        planes[slot, 0, q] = ((twice & 15) - less).astype(jnp.int8)
        planes[slot, 1, q] = ((twice >> 4) - less).astype(jnp.int8)


def count_block(planes, slot):
    zero = jnp.zeros((), F8)
    one = jnp.ones((), F8)
    digits = [jnp.int8(d) for d in range(0, 16, 2)]
    row = lax.broadcasted_iota(jnp.int32, (8, 128), 0)
    lane = lax.broadcasted_iota(jnp.int32, (8, 128), 1)
    second = (lane % 16) >= 8
    slot_of = lane // 16
    idx = (lane % 8) * 16 + ((lane // 8) % 2) * 8 + row
    low, high = [], []
    for q in range(8):
        lo, hi = planes[slot, 0, q], planes[slot, 1, q]
        lhs = jnp.concatenate([jnp.where(hi == d, one, zero) for d in digits], 0)
        rhs = jnp.concatenate([jnp.where(lo == d, one, zero) for d in digits], 0)
        out = lax.dot_general(lhs, rhs, (((1,), (1,)), ((), ())), preferred_element_type=F32)
        out = out[0:128] + 1024.0 * out[128:256]
        parts = []
        for m in range(2):
            part = None
            for h in range(8):
                at = 16 * h
                a = out[at : at + 8, 128 * m : 128 * m + 128]
                b = out[at + 8 : at + 16, 128 * m : 128 * m + 128]
                own = jnp.take_along_axis(jnp.where(second, b, a), idx, axis=1)
                part = own if h == 0 else jnp.where(slot_of == h, own, part)
            parts.append(part)
        for packed in (
            jnp.where(second, pltpu.roll(parts[1], 8, 1), parts[0]),
            jnp.where(second, parts[1], pltpu.roll(parts[0], 120, 1)),
        ):
            upper = jnp.floor(packed * (1.0 / 1024.0))
            low.append(packed - 1024.0 * upper)
            high.append(upper)
    return jnp.concatenate(low, 0), jnp.concatenate(high, 0)


def exact_dot(a, b):
    return jnp.dot(a, b, precision=lax.Precision.HIGHEST, preferred_element_type=F32)


def pick_lane(table, idx):
    low, high = table[:, 0:128], table[:, 128:256]
    parts = []
    for at in (0, 128):
        want = idx[:, at : at + 128]
        inner = want & 127
        a = jnp.take_along_axis(low, inner, axis=1)
        b = jnp.take_along_axis(high, inner, axis=1)
        parts.append(jnp.where(want >= 128, b, a))
    return jnp.concatenate(parts, 1)


def make_table(day_total, tot, zone, reg, wid, off, out):
    me = lax.axis_index("tm")
    first = lax.rem(me, 128 // ROWS) * ROWS
    eye = lax.broadcasted_iota(jnp.int32, (ROWS, 128), 1) == first + lax.broadcasted_iota(
        jnp.int32, (ROWS, 128), 0
    )

    def column(ref, zero):
        line = jnp.broadcast_to(ref[pl.ds(me // (128 // ROWS), 1), :], (ROWS, 128))
        return jnp.sum(jnp.where(eye, line, zero), axis=1, keepdims=True)

    region = column(reg, 0)
    width = column(wid, 0.0)
    offset = column(off, 0.0)
    pick = (lax.broadcasted_iota(jnp.int32, (ROWS, REGIONS), 1) == region).astype(F32)
    upper = (
        lax.broadcasted_iota(jnp.int32, (BINS, BINS), 0)
        <= lax.broadcasted_iota(jnp.int32, (BINS, BINS), 1)
    ).astype(F32)
    pooled, stacked = [], []
    for s in range(3):
        mine = exact_dot(pick, jnp.concatenate([zone[s, k].reshape(REGIONS, 128) for k in range(NK)], 1))
        share = mine / jnp.sum(mine, axis=1, keepdims=True)
        pooled.append(tot[s] + POOL_WEIGHT * day_total * share)
    filled = [pooled[s] / jnp.maximum(pooled[s], 1.0) for s in range(2)]
    sums = exact_dot(jnp.concatenate(pooled + filled, 0), upper)
    ends = [sums[ROWS * s : ROWS * s + ROWS] for s in range(5)]
    rank = ends[2] - pooled[2] + 0.5 * pooled[2]
    quantile = []
    for s in range(2):
        at = jnp.zeros((ROWS, BINS), jnp.int32)
        for bit in (128, 64, 32, 16, 8, 4, 2, 1):
            full = pick_lane(ends[s], at + (bit - 1)) <= rank
            at = jnp.where(full, at + bit, at)
        at = jnp.minimum(at, BINS - 1)
        before = pick_lane(ends[s] - pooled[s], at)
        size = pick_lane(pooled[s], at)
        inside = jnp.minimum(jnp.maximum(rank - before, 0.0), size) / jnp.maximum(size, 1.0)
        quantile.append(pick_lane(ends[3 + s] - filled[s], at) + inside)
    centers = lax.broadcasted_iota(jnp.int32, (ROWS, BINS), 1).astype(F32) + 0.5
    out[...] = offset + width * ((centers + quantile[1]) - quantile[0])


def place():
    me = lax.axis_index("tm")
    k = lax.rem(me, NK)
    x = lax.rem(me // NK, NX)
    z = me // (NK * NX)
    return z, x, k


def tm_of(z, x, k):
    return (z * NX + x) * NK + k


def remote(src, dst, send, recv, tm, cells=None):
    target = {"tm": tm} if cells is None else {"tm": tm, "cells": cells}
    return pltpu.make_async_remote_copy(
        src_ref=src,
        dst_ref=dst,
        send_sem=send,
        recv_sem=recv,
        device_id=target,
        device_id_type=pl.DeviceIdType.MESH,
    )


def greet(partners):
    barrier = pltpu.get_barrier_semaphore()
    for target in partners:
        pl.semaphore_signal(
            barrier, inc=1, device_id=target, device_id_type=pl.DeviceIdType.MESH
        )
    return lambda: pl.semaphore_wait(barrier, len(partners))


def main_kernel(
    day_total, hist, obs, fut, reg_in, wid_in, off_in, table, fut_t, reg, wid, off,
    xbuf, planes, cnt, zin, core_in, acc, far_in, side_in, done, last_in, tot,
    zone, z_core, z_acc, z_x, z_acc2, z_z,
    s_in, s_core, r_core, s_far, r_far, s_side, r_side, s_last, r_last,
    zs_core, zr_core, zs_x, zr_x, zs_z, zr_z, zs_gx, zr_gx, zs_gk, zr_gk,
    gs_z, gr_z, gs_r, gr_r, gs_l, gr_l, gs_f, gr_f, gs_k, gr_k,
):
    z, x, k = place()
    c = lax.axis_index("cells")
    tm = lax.axis_index("tm")
    other = tm_of(z, x, 1 - k)
    right = lax.rem(x + 1, NX)
    left = lax.rem(x + NX - 1, NX)
    across = lax.rem(x + 2, NX)
    to_right, to_left = tm_of(z, right, k), tm_of(z, left, k)
    order = (across, right, left, x)

    lead = pltpu.make_async_copy(hist.at[:, 0:128], xbuf.at[0, :, 0:128], s_in.at[0])
    lead.start()
    small = [
        pltpu.make_async_copy(ref, to, s_in.at[4 + i])
        for i, (ref, to) in enumerate(((reg_in, reg), (wid_in, wid), (off_in, off)))
    ]
    small[0].start()
    series = [pltpu.make_async_copy(hist.at[:, 128:], xbuf.at[0, :, 128:], s_in.at[1])]
    series += [
        pltpu.make_async_copy(ref, xbuf.at[s], s_in.at[1 + s]) for s, ref in ((1, obs), (2, fut))
    ]
    for copy in series + small[1:]:
        copy.start()
    y, z_hi = c // 2, lax.rem(c, 2)
    z_full = z_hi * NZ + z
    plane = x * 4 + y
    across_plane = [lax.rem(plane + j, 16) for j in range(1, 16)]
    in_plane = [(tm_of(z, at // 4, k), lax.rem(at, 4) * 2 + z_hi) for at in across_plane]
    along_z = []
    for j in range(1, 2 * NZ):
        at = lax.rem(z_full + j, 2 * NZ)
        along_z.append((tm_of(lax.rem(at, NZ), x, k), y * 2 + at // NZ))
    partners = [{"tm": other}]
    partners += [{"tm": a, "cells": b} for a, b in in_plane + along_z]
    met = greet(partners)
    zin[...] = jnp.zeros_like(zin)

    blocks = xbuf.shape[2] // 128
    last_block = 3 * blocks - 1

    def stage(n):
        j = lax.rem(n, blocks)
        at = pl.ds(pl.multiple_of(j * 128, 128), 128)
        stage_block(xbuf[n // blocks, :, at], planes, lax.rem(n, 2))

    def count(first, stop):
        def one(n, carry):
            stage(jnp.minimum(n + 1, last_block))
            s = n // blocks
            j = lax.rem(n, blocks)
            zones = lax.broadcasted_iota(jnp.int32, (REGIONS, 128), 0)
            pick = (zones == reg[pl.ds(j, 1), :]).astype(BF16)
            counts = count_block(planes, lax.rem(n, 2))
            heads, rests = [], []
            for half, part in enumerate(counts):
                cnt[s, j // 2, pl.ds(lax.rem(j, 2) * 2, 2), :, :, 128 * half : 128 * half + 128] = (
                    part.reshape(2, NK, ROWS, 128)
                )
                head = jnp.minimum(part, 256.0)
                heads.append(head.astype(BF16))
                rests.append((part - head).astype(BF16))
            both = jnp.concatenate(
                [jnp.concatenate(heads, 1), jnp.concatenate(rests, 1)], 0
            )
            sums = jnp.dot(
                jnp.concatenate([pick, pick], 1), both, preferred_element_type=F32
            )
            zin[s, 0] += sums[:, 0:128]
            zin[s, 1] += sums[:, 128:256]
            return carry

        lax.fori_loop(first, stop, one, 0)

    started = []

    def run(copies):
        for copy in copies:
            copy.start()
        started.extend(copies)
        return copies

    held = {}

    def p0(s):
        held["zc", s] = run([remote(zin.at[s, 1 - k], z_core.at[s], zs_core.at[s], zr_core.at[s], other)])
        held["core", s] = run(
            [
                remote(cnt.at[s, :, at, 1 - k], core_in.at[s, j], s_core.at[s, j], r_core.at[s, j], other)
                for j, at in enumerate(order)
            ]
        )

    def p1(s):
        core = held["core", s]
        core[0].wait_recv()
        acc[s, 0] = cnt[s, :, across, k] + core_in[s, 0]
        held["far", s] = run(
            [
                remote(acc.at[s, 0, 0:2], far_in.at[s, 0], s_far.at[s, 0], r_far.at[s, 0], to_right),
                remote(acc.at[s, 0, 2:4], far_in.at[s, 1], s_far.at[s, 1], r_far.at[s, 1], to_left),
            ]
        )
        core[1].wait_recv()
        acc[s, 1, 2:4] = cnt[s, 2:4, right, k] + core_in[s, 1, 2:4]
        core[2].wait_recv()
        acc[s, 2, 0:2] = cnt[s, 0:2, left, k] + core_in[s, 2, 0:2]
        held["side", s] = run(
            [
                remote(acc.at[s, 1, 2:4], side_in.at[s, 0, 2:4], s_side.at[s, 0], r_side.at[s, 0], to_right),
                remote(acc.at[s, 2, 0:2], side_in.at[s, 1, 0:2], s_side.at[s, 1], r_side.at[s, 1], to_left),
            ]
        )
        core[3].wait_recv()
        acc[s, 3] = cnt[s, :, x, k] + core_in[s, 3]

    def p2(s):
        far = held["far", s]
        far[0].wait_recv()
        acc[s, 1, 0:2] = cnt[s, 0:2, right, k] + core_in[s, 1, 0:2] + far_in[s, 0]
        far[1].wait_recv()
        acc[s, 2, 2:4] = cnt[s, 2:4, left, k] + core_in[s, 2, 2:4] + far_in[s, 1]
        held["side", s] += run(
            [
                remote(acc.at[s, 1, 0:2], side_in.at[s, 0, 0:2], s_side.at[s, 2], r_side.at[s, 2], to_right),
                remote(acc.at[s, 2, 2:4], side_in.at[s, 1, 2:4], s_side.at[s, 3], r_side.at[s, 3], to_left),
            ]
        )

    def p3(s):
        for copy in held["side", s]:
            copy.wait_recv()
        done[s] = acc[s, 3] + side_in[s, 0] + side_in[s, 1]
        held["last", s] = run(
            [
                remote(done.at[s, lax.rem(z + j, NZ)], last_in.at[s, j - 1], s_last.at[s, j - 1],
                       r_last.at[s, j - 1], tm_of(lax.rem(z + j, NZ), x, k))
                for j in range(1, NZ)
            ]
        )

    def p4(s):
        for copy in held["last", s]:
            copy.wait_recv()
        tot[s] = done[s, z] + last_in[s, 0] + last_in[s, 1] + last_in[s, 2]

    def q1(s):
        held["zc", s][0].wait_recv()
        z_acc[s] = (zin[s, k] + z_core[s]).reshape(16, 8, 128)
        held["zx", s] = run(
            [
                remote(z_acc.at[s, at], z_x.at[s, j], zs_x.at[s, j], zr_x.at[s, j], *in_plane[j])
                for j, at in enumerate(across_plane)
            ]
        )

    def q2(s):
        for copy in held["zx", s]:
            copy.wait_recv()
        total = z_acc[s, plane]
        for j in range(15):
            total = total + z_x[s, j]
        z_acc2[s] = total

    def q3(s):
        held["zz", s] = run(
            [
                remote(z_acc2.at[s], z_z.at[s, j], zs_z.at[s, j], zr_z.at[s, j], *at)
                for j, at in enumerate(along_z)
            ]
        )

    def q4(s):
        for copy in held["zz", s]:
            copy.wait_recv()
        total = z_acc2[s]
        for j in range(2 * NZ - 1):
            total = total + z_z[s, j]
        zone[s, k, plane] = total

    def q5(s):
        held["gx", s] = run(
            [
                remote(zone.at[s, k, plane], zone.at[s, k, plane], zs_gx.at[s, j], zr_gx.at[s, j], *at)
                for j, at in enumerate(in_plane)
            ]
        )

    def q55(s):
        for copy in held["gx", s]:
            copy.wait_recv()
        held["gk", s] = run([remote(zone.at[s, k], zone.at[s, k], zs_gk.at[s], zr_gk.at[s], other)])

    def q6(s):
        held["gk", s][0].wait_recv()

    def turn(first, stop):
        for j in range(first, stop):
            fut_t[128 * j : 128 * j + 128, :] = xbuf[2, :, 128 * j : 128 * j + 128].T

    step = blocks // 4
    lead.wait()
    stage(jnp.int32(0))
    small[0].wait()
    series[0].wait()
    count(0, step)
    series[1].wait()
    count(step, blocks)
    met()
    p0(0)
    for s in (1, 2):
        first = s * blocks
        if s == 1:
            series[2].wait()
        count(first, first + step)
        if s == 2:
            p4(0)
        q1(s - 1)
        p1(s - 1)
        count(first + step, first + 2 * step)
        if s == 2:
            q55(0)
        q2(s - 1)
        q3(s - 1)
        p2(s - 1)
        count(first + 2 * step, first + 3 * step)
        if s == 2:
            q6(0)
        p3(s - 1)
        count(first + 3 * step, first + blocks)
        p0(s)
        q4(s - 1)
        q5(s - 1)
    q1(2)
    p1(2)
    p4(1)
    turn(0, 4)
    q2(2)
    q3(2)
    p2(2)
    q55(1)
    turn(4, blocks)
    p3(2)
    q4(2)
    q5(2)
    p4(2)
    q6(1)
    small[1].wait()
    small[2].wait()
    q55(2)
    q6(2)

    make_table(day_total, tot, zone, reg, wid, off, table.at[z, x, k])

    def piece(z_at, x_at):
        return table.at[z_at, x_at, k]

    def spread(j, z_at):
        held["r", j] = run([remote(piece(z_at, x), piece(z_at, x), gs_r.at[j], gr_r.at[j], to_right)])[0]
        held["l", j] = run([remote(piece(z_at, x), piece(z_at, x), gs_l.at[j], gr_l.at[j], to_left)])[0]
        held["k", j] = run([remote(piece(z_at, x), piece(z_at, x), gs_k.at[j], gr_k.at[j], other)])[0]

    zs = run(
        [
            remote(piece(z, x), piece(z, x), gs_z.at[j - 1], gr_z.at[j - 1],
                   tm_of(lax.rem(z + j, NZ), x, k))
            for j in range(1, NZ)
        ]
    )
    spread(0, z)
    back = [lax.rem(z + NZ - j, NZ) for j in range(NZ)]
    passed = lax.rem(x + NX - 1 + 2 * k, NX)
    onward = tm_of(z, lax.rem(x + 1 + 2 * k, NX), k)

    def relay(j):
        held["r", j].wait_recv()
        held["l", j].wait_recv()
        z_at = back[j]
        held["f", j] = run([remote(piece(z_at, passed), piece(z_at, passed), gs_f.at[j], gr_f.at[j], onward)])[0]
        for i, at in enumerate((left, right)):
            n = 4 + 4 * i + j
            held["k", n] = run([remote(piece(z_at, at), piece(z_at, at), gs_k.at[n], gr_k.at[n], other)])[0]

    def finish(j):
        held["f", j].wait_recv()
        z_at = back[j]
        held["k", 12 + j] = run(
            [remote(piece(z_at, across), piece(z_at, across), gs_k.at[12 + j], gr_k.at[12 + j], other)]
        )[0]

    zs[0].wait_recv()
    spread(1, back[1])
    relay(0)
    zs[1].wait_recv()
    spread(2, back[2])
    zs[2].wait_recv()
    spread(3, back[3])
    relay(1)
    finish(0)
    relay(2)
    finish(1)
    relay(3)
    finish(2)
    finish(3)
    for j in range(4 * NZ):
        held["k", j].wait_recv()
    for copy in started:
        copy.wait_send()


def map_table(hist_bin, obs_bin, fut_bin, region, width, offset, day_total):
    days, cells = hist_bin.shape
    vmem = pl.BlockSpec(memory_space=pltpu.VMEM)
    hbm = pl.BlockSpec(memory_space=pltpu.HBM)
    dma = pltpu.SemaphoreType.DMA
    block = (NZ, ROWS, BINS)
    small = (8, 128)
    return pl.pallas_call(
        functools.partial(main_kernel, float(day_total)),
        out_shape=(
            jax.ShapeDtypeStruct((NZ, NX, NK, ROWS, BINS), F32),
            jax.ShapeDtypeStruct((cells, days), jnp.int32),
        ),
        in_specs=[hbm] * 6,
        out_specs=(vmem, vmem),
        scratch_shapes=[
            pltpu.VMEM((8, 128), jnp.int32),
            pltpu.VMEM((8, 128), F32),
            pltpu.VMEM((8, 128), F32),
            pltpu.VMEM((3, days, cells), jnp.int32),
            pltpu.VMEM((2, 2, 8, 32, days), jnp.int8),
            pltpu.VMEM((3, NZ, NX, NK, ROWS, BINS), F32),
            pltpu.VMEM((3, NK, REGIONS, 128), F32),
            pltpu.VMEM((3, 4, *block), F32),
            pltpu.VMEM((3, 4, *block), F32),
            pltpu.VMEM((3, 2, 2, ROWS, BINS), F32),
            pltpu.VMEM((3, 2, *block), F32),
            pltpu.VMEM((3, *block), F32),
            pltpu.VMEM((3, 3, ROWS, BINS), F32),
            pltpu.VMEM((3, ROWS, BINS), F32),
            pltpu.VMEM((3, NK, 16, *small), F32),
            pltpu.VMEM((3, REGIONS, 128), F32),
            pltpu.VMEM((3, 16, *small), F32),
            pltpu.VMEM((3, 15, *small), F32),
            pltpu.VMEM((3, *small), F32),
            pltpu.VMEM((3, 7, *small), F32),
            dma((7,)),
            dma((3, 4)), dma((3, 4)), dma((3, 2)), dma((3, 2)), dma((3, 4)), dma((3, 4)), dma((3, 3)), dma((3, 3)),
            dma((3,)), dma((3,)), dma((3, 15)), dma((3, 15)), dma((3, 7)), dma((3, 7)),
            dma((3, 15)), dma((3, 15)), dma((3,)), dma((3,)),
            dma((3,)), dma((3,)), dma((4,)), dma((4,)), dma((4,)), dma((4,)), dma((4,)), dma((4,)),
            dma((16,)), dma((16,)),
        ],
        compiler_params=pltpu.CompilerParams(
            collective_id=0, has_side_effects=True, vmem_limit_bytes=58 * 2**20
        ),
        name="map_table",
    )(hist_bin, obs_bin, fut_bin, *(a.reshape(-1, 128) for a in (region, width, offset)))


APPLY = 256


def apply_kernel(x_ref, t_ref, o_ref):
    rows = pl.ds(pl.multiple_of(pl.program_id(0) * APPLY, APPLY), APPLY)
    low = t_ref[rows, 0:128]
    high = t_ref[rows, 128:256]
    for at in range(0, x_ref.shape[1], 128):
        idx = x_ref[rows, at : at + 128]
        inner = idx & 127
        a = jnp.take_along_axis(low, inner, axis=1)
        b = jnp.take_along_axis(high, inner, axis=1)
        o_ref[at : at + 128, :] = jnp.where(idx >= 128, b, a).T


def apply_table(fut_t, table):
    cells, days = fut_t.shape
    vmem = pl.BlockSpec(memory_space=pltpu.VMEM)
    return pl.pallas_call(
        apply_kernel,
        grid=(cells // APPLY,),
        in_specs=[vmem, vmem],
        out_specs=pl.BlockSpec((days, APPLY), lambda j: (0, j)),
        out_shape=jax.ShapeDtypeStruct((days, cells), F32),
        name="apply",
    )(fut_t, table)


def body(hist_bin, obs_bin, fut_bin, region_id, bin_width, bin_offset):
    days = hist_bin.shape[0] * lax.axis_size("tm")
    table, fut_t = map_table(hist_bin, obs_bin, fut_bin, region_id, bin_width, bin_offset, days)
    return apply_table(fut_t, table.reshape(-1, BINS))


def solution(mesh):
    placed = (
        P("tm", "cells"),
        P("tm", "cells"),
        P("tm", "cells"),
        P("cells"),
        P("cells"),
        P("cells"),
    )
    return jax.shard_map(
        body, mesh=mesh, in_specs=placed, out_specs=P("tm", "cells"), check_vma=False
    )
```

```python
import functools

import jax
import jax.numpy as jnp
from jax import lax
from jax.experimental import pallas as pl
from jax.experimental.pallas import tpu as pltpu
from jax.sharding import PartitionSpec as P

BINS = 256
REGIONS = 128
F32 = jnp.float32
BF16 = jnp.bfloat16
F8 = jnp.float8_e4m3fn
POOL_WEIGHT = 0.5

NZ, NX, NK = 4, 4, 2
NC = 8
ROWS = 32


def stage_block(bins, planes, slot):
    xt = bins.T
    less = (lax.broadcasted_iota(jnp.int32, (32, bins.shape[0]), 0) >= 16).astype(jnp.int32)
    for q in range(8):
        rows = xt[16 * q : 16 * q + 16]
        twice = jnp.concatenate([rows, rows], 0)
        planes[slot, 0, q] = ((twice & 15) - less).astype(jnp.int8)
        planes[slot, 1, q] = ((twice >> 4) - less).astype(jnp.int8)


def count_block(planes, slot):
    zero = jnp.zeros((), F8)
    one = jnp.ones((), F8)
    digits = [jnp.int8(d) for d in range(0, 16, 2)]
    row = lax.broadcasted_iota(jnp.int32, (8, 128), 0)
    lane = lax.broadcasted_iota(jnp.int32, (8, 128), 1)
    second = (lane % 16) >= 8
    slot_of = lane // 16
    idx = (lane % 8) * 16 + ((lane // 8) % 2) * 8 + row
    low, high = [], []
    for q in range(8):
        lo, hi = planes[slot, 0, q], planes[slot, 1, q]
        lhs = jnp.concatenate([jnp.where(hi == d, one, zero) for d in digits], 0)
        rhs = jnp.concatenate([jnp.where(lo == d, one, zero) for d in digits], 0)
        out = lax.dot_general(lhs, rhs, (((1,), (1,)), ((), ())), preferred_element_type=F32)
        out = out[0:128] + 1024.0 * out[128:256]
        parts = []
        for m in range(2):
            part = None
            for h in range(8):
                at = 16 * h
                a = out[at : at + 8, 128 * m : 128 * m + 128]
                b = out[at + 8 : at + 16, 128 * m : 128 * m + 128]
                own = jnp.take_along_axis(jnp.where(second, b, a), idx, axis=1)
                part = own if h == 0 else jnp.where(slot_of == h, own, part)
            parts.append(part)
        for packed in (
            jnp.where(second, pltpu.roll(parts[1], 8, 1), parts[0]),
            jnp.where(second, parts[1], pltpu.roll(parts[0], 120, 1)),
        ):
            upper = jnp.floor(packed * (1.0 / 1024.0))
            low.append(packed - 1024.0 * upper)
            high.append(upper)
    return jnp.concatenate(low, 0), jnp.concatenate(high, 0)


def exact_dot(a, b):
    return jnp.dot(a, b, precision=lax.Precision.HIGHEST, preferred_element_type=F32)


def pick_lane(table, idx):
    low, high = table[:, 0:128], table[:, 128:256]
    parts = []
    for at in (0, 128):
        want = idx[:, at : at + 128]
        inner = want & 127
        a = jnp.take_along_axis(low, inner, axis=1)
        b = jnp.take_along_axis(high, inner, axis=1)
        parts.append(jnp.where(want >= 128, b, a))
    return jnp.concatenate(parts, 1)


def make_table(day_total, tot, zone, reg, wid, off, out):
    me = lax.axis_index("tm")
    first = lax.rem(me, 128 // ROWS) * ROWS
    eye = lax.broadcasted_iota(jnp.int32, (ROWS, 128), 1) == first + lax.broadcasted_iota(
        jnp.int32, (ROWS, 128), 0
    )

    def column(ref, zero):
        line = jnp.broadcast_to(ref[pl.ds(me // (128 // ROWS), 1), :], (ROWS, 128))
        return jnp.sum(jnp.where(eye, line, zero), axis=1, keepdims=True)

    region = column(reg, 0)
    width = column(wid, 0.0)
    offset = column(off, 0.0)
    pick = (lax.broadcasted_iota(jnp.int32, (ROWS, REGIONS), 1) == region).astype(F32)
    upper = (
        lax.broadcasted_iota(jnp.int32, (BINS, BINS), 0)
        <= lax.broadcasted_iota(jnp.int32, (BINS, BINS), 1)
    ).astype(F32)
    pooled, stacked = [], []
    for s in range(3):
        mine = exact_dot(pick, jnp.concatenate([zone[s, k].reshape(REGIONS, 128) for k in range(NK)], 1))
        share = mine / jnp.sum(mine, axis=1, keepdims=True)
        pooled.append(tot[s] + POOL_WEIGHT * day_total * share)
    filled = [pooled[s] / jnp.maximum(pooled[s], 1.0) for s in range(2)]
    sums = exact_dot(jnp.concatenate(pooled + filled, 0), upper)
    ends = [sums[ROWS * s : ROWS * s + ROWS] for s in range(5)]
    rank = ends[2] - pooled[2] + 0.5 * pooled[2]
    quantile = []
    for s in range(2):
        at = jnp.zeros((ROWS, BINS), jnp.int32)
        for bit in (128, 64, 32, 16, 8, 4, 2, 1):
            full = pick_lane(ends[s], at + (bit - 1)) <= rank
            at = jnp.where(full, at + bit, at)
        at = jnp.minimum(at, BINS - 1)
        before = pick_lane(ends[s] - pooled[s], at)
        size = pick_lane(pooled[s], at)
        inside = jnp.minimum(jnp.maximum(rank - before, 0.0), size) / jnp.maximum(size, 1.0)
        quantile.append(pick_lane(ends[3 + s] - filled[s], at) + inside)
    centers = lax.broadcasted_iota(jnp.int32, (ROWS, BINS), 1).astype(F32) + 0.5
    out[...] = offset + width * ((centers + quantile[1]) - quantile[0])


def place():
    me = lax.axis_index("tm")
    k = lax.rem(me, NK)
    x = lax.rem(me // NK, NX)
    z = me // (NK * NX)
    return z, x, k


def tm_of(z, x, k):
    return (z * NX + x) * NK + k


def remote(src, dst, send, recv, tm, cells=None):
    target = {"tm": tm} if cells is None else {"tm": tm, "cells": cells}
    return pltpu.make_async_remote_copy(
        src_ref=src,
        dst_ref=dst,
        send_sem=send,
        recv_sem=recv,
        device_id=target,
        device_id_type=pl.DeviceIdType.MESH,
    )


def greet(partners):
    barrier = pltpu.get_barrier_semaphore()
    for target in partners:
        pl.semaphore_signal(
            barrier, inc=1, device_id=target, device_id_type=pl.DeviceIdType.MESH
        )
    return lambda: pl.semaphore_wait(barrier, len(partners))


def main_kernel(
    day_total, hist, obs, fut, reg_in, wid_in, off_in, table, fut_t, reg, wid, off,
    xbuf, planes, cnt, zin, core_in, acc, far_in, side_in, done, last_in, tot,
    zone, z_core, z_acc, z_x, z_acc2, z_z,
    s_in, s_core, r_core, s_far, r_far, s_side, r_side, s_last, r_last,
    zs_core, zr_core, zs_x, zr_x, zs_z, zr_z, zs_gx, zr_gx, zs_gk, zr_gk,
    gs_z, gr_z, gs_r, gr_r, gs_l, gr_l, gs_f, gr_f, gs_k, gr_k,
):
    z, x, k = place()
    c = lax.axis_index("cells")
    tm = lax.axis_index("tm")
    other = tm_of(z, x, 1 - k)
    right = lax.rem(x + 1, NX)
    left = lax.rem(x + NX - 1, NX)
    across = lax.rem(x + 2, NX)
    to_right, to_left = tm_of(z, right, k), tm_of(z, left, k)
    order = (across, right, left, x)

    lead = pltpu.make_async_copy(hist.at[:, 0:128], xbuf.at[0, :, 0:128], s_in.at[0])
    lead.start()
    small = [
        pltpu.make_async_copy(ref, to, s_in.at[4 + i])
        for i, (ref, to) in enumerate(((reg_in, reg), (wid_in, wid), (off_in, off)))
    ]
    small[0].start()
    series = [pltpu.make_async_copy(hist.at[:, 128:], xbuf.at[0, :, 128:], s_in.at[1])]
    series += [
        pltpu.make_async_copy(ref, xbuf.at[s], s_in.at[1 + s]) for s, ref in ((1, obs), (2, fut))
    ]
    for copy in series + small[1:]:
        copy.start()
    y, z_hi = c // 2, lax.rem(c, 2)
    z_full = z_hi * NZ + z
    plane = x * 4 + y
    across_plane = [lax.rem(plane + j, 16) for j in range(1, 16)]
    in_plane = [(tm_of(z, at // 4, k), lax.rem(at, 4) * 2 + z_hi) for at in across_plane]
    along_z = []
    for j in range(1, 2 * NZ):
        at = lax.rem(z_full + j, 2 * NZ)
        along_z.append((tm_of(lax.rem(at, NZ), x, k), y * 2 + at // NZ))
    partners = [{"tm": other}]
    partners += [{"tm": a, "cells": b} for a, b in in_plane + along_z]
    met = greet(partners)
    zin[...] = jnp.zeros_like(zin)

    blocks = xbuf.shape[2] // 128
    last_block = 3 * blocks - 1

    def stage(n):
        j = lax.rem(n, blocks)
        at = pl.ds(pl.multiple_of(j * 128, 128), 128)
        stage_block(xbuf[n // blocks, :, at], planes, lax.rem(n, 2))

    def count(first, stop):
        def one(n, carry):
            stage(jnp.minimum(n + 1, last_block))
            s = n // blocks
            j = lax.rem(n, blocks)
            zones = lax.broadcasted_iota(jnp.int32, (REGIONS, 128), 0)
            pick = (zones == reg[pl.ds(j, 1), :]).astype(BF16)
            counts = count_block(planes, lax.rem(n, 2))
            heads, rests = [], []
            for half, part in enumerate(counts):
                cnt[s, j // 2, pl.ds(lax.rem(j, 2) * 2, 2), :, :, 128 * half : 128 * half + 128] = (
                    part.reshape(2, NK, ROWS, 128)
                )
                head = jnp.minimum(part, 256.0)
                heads.append(head.astype(BF16))
                rests.append((part - head).astype(BF16))
            both = jnp.concatenate(
                [jnp.concatenate(heads, 1), jnp.concatenate(rests, 1)], 0
            )
            sums = jnp.dot(
                jnp.concatenate([pick, pick], 1), both, preferred_element_type=F32
            )
            zin[s, 0] += sums[:, 0:128]
            zin[s, 1] += sums[:, 128:256]
            return carry

        lax.fori_loop(first, stop, one, 0)

    started = []

    def run(copies):
        for copy in copies:
            copy.start()
        started.extend(copies)
        return copies

    held = {}

    def p0(s):
        held["zc", s] = run([remote(zin.at[s, 1 - k], z_core.at[s], zs_core.at[s], zr_core.at[s], other)])
        held["core", s] = run(
            [
                remote(cnt.at[s, :, at, 1 - k], core_in.at[s, j], s_core.at[s, j], r_core.at[s, j], other)
                for j, at in enumerate(order)
            ]
        )

    def p1(s):
        core = held["core", s]
        core[0].wait_recv()
        acc[s, 0] = cnt[s, :, across, k] + core_in[s, 0]
        held["far", s] = run(
            [
                remote(acc.at[s, 0, 0:2], far_in.at[s, 0], s_far.at[s, 0], r_far.at[s, 0], to_right),
                remote(acc.at[s, 0, 2:4], far_in.at[s, 1], s_far.at[s, 1], r_far.at[s, 1], to_left),
            ]
        )
        core[1].wait_recv()
        acc[s, 1, 2:4] = cnt[s, 2:4, right, k] + core_in[s, 1, 2:4]
        core[2].wait_recv()
        acc[s, 2, 0:2] = cnt[s, 0:2, left, k] + core_in[s, 2, 0:2]
        held["side", s] = run(
            [
                remote(acc.at[s, 1, 2:4], side_in.at[s, 0, 2:4], s_side.at[s, 0], r_side.at[s, 0], to_right),
                remote(acc.at[s, 2, 0:2], side_in.at[s, 1, 0:2], s_side.at[s, 1], r_side.at[s, 1], to_left),
            ]
        )
        core[3].wait_recv()
        acc[s, 3] = cnt[s, :, x, k] + core_in[s, 3]

    def p2(s):
        far = held["far", s]
        far[0].wait_recv()
        acc[s, 1, 0:2] = cnt[s, 0:2, right, k] + core_in[s, 1, 0:2] + far_in[s, 0]
        far[1].wait_recv()
        acc[s, 2, 2:4] = cnt[s, 2:4, left, k] + core_in[s, 2, 2:4] + far_in[s, 1]
        held["side", s] += run(
            [
                remote(acc.at[s, 1, 0:2], side_in.at[s, 0, 0:2], s_side.at[s, 2], r_side.at[s, 2], to_right),
                remote(acc.at[s, 2, 2:4], side_in.at[s, 1, 2:4], s_side.at[s, 3], r_side.at[s, 3], to_left),
            ]
        )

    def p3(s):
        for copy in held["side", s]:
            copy.wait_recv()
        done[s] = acc[s, 3] + side_in[s, 0] + side_in[s, 1]
        held["last", s] = run(
            [
                remote(done.at[s, lax.rem(z + j, NZ)], last_in.at[s, j - 1], s_last.at[s, j - 1],
                       r_last.at[s, j - 1], tm_of(lax.rem(z + j, NZ), x, k))
                for j in range(1, NZ)
            ]
        )

    def p4(s):
        for copy in held["last", s]:
            copy.wait_recv()
        tot[s] = done[s, z] + last_in[s, 0] + last_in[s, 1] + last_in[s, 2]

    def q1(s):
        held["zc", s][0].wait_recv()
        z_acc[s] = (zin[s, k] + z_core[s]).reshape(16, 8, 128)
        held["zx", s] = run(
            [
                remote(z_acc.at[s, at], z_x.at[s, j], zs_x.at[s, j], zr_x.at[s, j], *in_plane[j])
                for j, at in enumerate(across_plane)
            ]
        )

    def q2(s):
        for copy in held["zx", s]:
            copy.wait_recv()
        total = z_acc[s, plane]
        for j in range(15):
            total = total + z_x[s, j]
        z_acc2[s] = total

    def q3(s):
        held["zz", s] = run(
            [
                remote(z_acc2.at[s], z_z.at[s, j], zs_z.at[s, j], zr_z.at[s, j], *at)
                for j, at in enumerate(along_z)
            ]
        )

    def q4(s):
        for copy in held["zz", s]:
            copy.wait_recv()
        total = z_acc2[s]
        for j in range(2 * NZ - 1):
            total = total + z_z[s, j]
        zone[s, k, plane] = total

    def q5(s):
        held["gx", s] = run(
            [
                remote(zone.at[s, k, plane], zone.at[s, k, plane], zs_gx.at[s, j], zr_gx.at[s, j], *at)
                for j, at in enumerate(in_plane)
            ]
        )

    def q55(s):
        for copy in held["gx", s]:
            copy.wait_recv()
        held["gk", s] = run([remote(zone.at[s, k], zone.at[s, k], zs_gk.at[s], zr_gk.at[s], other)])

    def q6(s):
        held["gk", s][0].wait_recv()

    def turn(first, stop):
        for j in range(first, stop):
            fut_t[128 * j : 128 * j + 128, :] = xbuf[2, :, 128 * j : 128 * j + 128].T

    half = blocks // 2
    lead.wait()
    stage(jnp.int32(0))
    small[0].wait()
    series[0].wait()
    count(0, half)
    series[1].wait()
    count(half, 2 * half)
    met()
    p0(0)
    count(2 * half, 3 * half)
    q1(0)
    p1(0)
    series[2].wait()
    count(3 * half, 4 * half)
    p0(1)
    q2(0)
    q3(0)
    p2(0)
    count(4 * half, 5 * half)
    q1(1)
    p1(1)
    q4(0)
    q5(0)
    p3(0)
    count(5 * half, 6 * half)
    p0(2)
    q2(1)
    q3(1)
    p2(1)
    q1(2)
    p1(2)
    q55(0)
    p4(0)
    turn(0, half)
    q2(2)
    q3(2)
    p2(2)
    p3(1)
    q4(1)
    q5(1)
    q6(0)
    turn(half, blocks)
    p3(2)
    q4(2)
    q5(2)
    q55(1)
    p4(1)
    p4(2)
    small[1].wait()
    small[2].wait()
    q6(1)
    q55(2)
    q6(2)

    make_table(day_total, tot, zone, reg, wid, off, table.at[z, x, k])

    def piece(z_at, x_at):
        return table.at[z_at, x_at, k]

    def spread(j, z_at):
        held["r", j] = run([remote(piece(z_at, x), piece(z_at, x), gs_r.at[j], gr_r.at[j], to_right)])[0]
        held["l", j] = run([remote(piece(z_at, x), piece(z_at, x), gs_l.at[j], gr_l.at[j], to_left)])[0]
        held["k", j] = run([remote(piece(z_at, x), piece(z_at, x), gs_k.at[j], gr_k.at[j], other)])[0]

    zs = run(
        [
            remote(piece(z, x), piece(z, x), gs_z.at[j - 1], gr_z.at[j - 1],
                   tm_of(lax.rem(z + j, NZ), x, k))
            for j in range(1, NZ)
        ]
    )
    spread(0, z)
    back = [lax.rem(z + NZ - j, NZ) for j in range(NZ)]
    passed = lax.rem(x + NX - 1 + 2 * k, NX)
    onward = tm_of(z, lax.rem(x + 1 + 2 * k, NX), k)

    def relay(j):
        held["r", j].wait_recv()
        held["l", j].wait_recv()
        z_at = back[j]
        held["f", j] = run([remote(piece(z_at, passed), piece(z_at, passed), gs_f.at[j], gr_f.at[j], onward)])[0]
        for i, at in enumerate((left, right)):
            n = 4 + 4 * i + j
            held["k", n] = run([remote(piece(z_at, at), piece(z_at, at), gs_k.at[n], gr_k.at[n], other)])[0]

    def finish(j):
        held["f", j].wait_recv()
        z_at = back[j]
        held["k", 12 + j] = run(
            [remote(piece(z_at, across), piece(z_at, across), gs_k.at[12 + j], gr_k.at[12 + j], other)]
        )[0]

    zs[0].wait_recv()
    spread(1, back[1])
    relay(0)
    zs[1].wait_recv()
    spread(2, back[2])
    zs[2].wait_recv()
    spread(3, back[3])
    relay(1)
    finish(0)
    relay(2)
    finish(1)
    relay(3)
    finish(2)
    finish(3)
    for j in range(4 * NZ):
        held["k", j].wait_recv()
    for copy in started:
        copy.wait_send()


def map_table(hist_bin, obs_bin, fut_bin, region, width, offset, day_total):
    days, cells = hist_bin.shape
    vmem = pl.BlockSpec(memory_space=pltpu.VMEM)
    hbm = pl.BlockSpec(memory_space=pltpu.HBM)
    dma = pltpu.SemaphoreType.DMA
    block = (NZ, ROWS, BINS)
    small = (8, 128)
    return pl.pallas_call(
        functools.partial(main_kernel, float(day_total)),
        out_shape=(
            jax.ShapeDtypeStruct((NZ, NX, NK, ROWS, BINS), F32),
            jax.ShapeDtypeStruct((cells, days), jnp.int32),
        ),
        in_specs=[hbm] * 6,
        out_specs=(vmem, vmem),
        scratch_shapes=[
            pltpu.VMEM((8, 128), jnp.int32),
            pltpu.VMEM((8, 128), F32),
            pltpu.VMEM((8, 128), F32),
            pltpu.VMEM((3, days, cells), jnp.int32),
            pltpu.VMEM((2, 2, 8, 32, days), jnp.int8),
            pltpu.VMEM((3, NZ, NX, NK, ROWS, BINS), F32),
            pltpu.VMEM((3, NK, REGIONS, 128), F32),
            pltpu.VMEM((3, 4, *block), F32),
            pltpu.VMEM((3, 4, *block), F32),
            pltpu.VMEM((3, 2, 2, ROWS, BINS), F32),
            pltpu.VMEM((3, 2, *block), F32),
            pltpu.VMEM((3, *block), F32),
            pltpu.VMEM((3, 3, ROWS, BINS), F32),
            pltpu.VMEM((3, ROWS, BINS), F32),
            pltpu.VMEM((3, NK, 16, *small), F32),
            pltpu.VMEM((3, REGIONS, 128), F32),
            pltpu.VMEM((3, 16, *small), F32),
            pltpu.VMEM((3, 15, *small), F32),
            pltpu.VMEM((3, *small), F32),
            pltpu.VMEM((3, 7, *small), F32),
            dma((7,)),
            dma((3, 4)), dma((3, 4)), dma((3, 2)), dma((3, 2)), dma((3, 4)), dma((3, 4)), dma((3, 3)), dma((3, 3)),
            dma((3,)), dma((3,)), dma((3, 15)), dma((3, 15)), dma((3, 7)), dma((3, 7)),
            dma((3, 15)), dma((3, 15)), dma((3,)), dma((3,)),
            dma((3,)), dma((3,)), dma((4,)), dma((4,)), dma((4,)), dma((4,)), dma((4,)), dma((4,)),
            dma((16,)), dma((16,)),
        ],
        compiler_params=pltpu.CompilerParams(
            collective_id=0, has_side_effects=True, vmem_limit_bytes=58 * 2**20
        ),
        name="map_table",
    )(hist_bin, obs_bin, fut_bin, *(a.reshape(-1, 128) for a in (region, width, offset)))


APPLY = 256


def apply_kernel(x_ref, t_ref, o_ref):
    rows = pl.ds(pl.multiple_of(pl.program_id(0) * APPLY, APPLY), APPLY)
    low = t_ref[rows, 0:128]
    high = t_ref[rows, 128:256]
    for at in range(0, x_ref.shape[1], 128):
        idx = x_ref[rows, at : at + 128]
        inner = idx & 127
        a = jnp.take_along_axis(low, inner, axis=1)
        b = jnp.take_along_axis(high, inner, axis=1)
        o_ref[at : at + 128, :] = jnp.where(idx >= 128, b, a).T


def apply_table(fut_t, table):
    cells, days = fut_t.shape
    vmem = pl.BlockSpec(memory_space=pltpu.VMEM)
    return pl.pallas_call(
        apply_kernel,
        grid=(cells // APPLY,),
        in_specs=[vmem, vmem],
        out_specs=pl.BlockSpec((days, APPLY), lambda j: (0, j)),
        out_shape=jax.ShapeDtypeStruct((days, cells), F32),
        name="apply",
    )(fut_t, table)


def body(hist_bin, obs_bin, fut_bin, region_id, bin_width, bin_offset):
    days = hist_bin.shape[0] * lax.axis_size("tm")
    table, fut_t = map_table(hist_bin, obs_bin, fut_bin, region_id, bin_width, bin_offset, days)
    return apply_table(fut_t, table.reshape(-1, BINS))


def solution(mesh):
    placed = (
        P("tm", "cells"),
        P("tm", "cells"),
        P("tm", "cells"),
        P("cells"),
        P("cells"),
        P("cells"),
    )
    return jax.shard_map(
        body, mesh=mesh, in_specs=placed, out_specs=P("tm", "cells"), check_vma=False
    )
```
